32 devices in a mesh: flow: 2 (over x), cross: 4 (over z), depth: 4 (over y, core).
Axes of the slice: x: 2, y: 2, z: 4, core: 2. Of those that a mesh axis runs over, the one named last changes fastest.
Arguments:
- fluid_offsets: float32 [3, 2, 16, 16, 128], P(None, 'flow', 'cross', 'depth'), may hold values from 0 to 1
- source: float32 [2, 16, 16, 128], P('flow', 'cross', 'depth'), may hold values from -6 to 6
- marker_offsets: float32 [512, 16, 3, 128], P(('flow', 'cross', 'depth')), may hold values from 0 to 1
- marker_normals: float32 [512, 16, 3, 128], P(('flow', 'cross', 'depth')), may hold values from -6 to 6
- dest_tile: int32 [512, 16, 1], P(('flow', 'cross', 'depth')), may hold values from 0 to 7; in each aligned block of 256 rows (0 to 255, 256 to 511, ..., all dimensions but the last counted through in order) at most 64 rows name the same one
- cell_index: int32 [512, 16], P(('flow', 'cross', 'depth')), may hold values from 0 to 15
- grain_velocity: float32 [512, 3], P(('flow', 'cross', 'depth')), may hold values from -6 to 6
- grain_mass: float32 [512], P(('flow', 'cross', 'depth')), may hold values from 0.5 to 4
Outputs:
- pressure: float32 [2, 16, 16, 128], P('flow', 'cross', 'depth')
- velocity_out: float32 [512, 3], P(('flow', 'cross', 'depth'))
The draws below stay inside these ranges and needn't reach their ends.
Inputs may be any that keep to these rules, and one draw needn't show every extreme that they name: `dest_tile`: in the rows of one device at most 64 marker blocks name the same tile.
All inputs are finite; a program needn't handle non-finite values.
Results may differ from the reference program's by a relative error of at most 0.0003.
Values sent between devices are 32-bit elements; how exact they have to be, the bound alone decides.
A program may use at most 64 MiB of HBM per device.

```python
import math
import jax
import jax.numpy as jnp
import numpy as np
from jax import lax

CX = 1
CY = 4
CZ = 4
G_DEV = 16
MB = 16
ITERS = 4
STEPS = 2
CELLS = 16
NX = 2
NY = 16
NZ = 16
GRAINS = 512
CAP = 64
N_FLOW = 2
N_CROSS = 4
N_DEPTH = 4


def touch_ends(values, stream_key, least, high):
    dims = values.shape
    spot = [jax.random.randint(jax.random.fold_in(stream_key, axis), (), 0, dims[axis]) for axis in range(len(dims))]
    values = values.at[tuple(spot)].set(least)
    longest = dims.index(max(dims))
    spot[longest] = (spot[longest] + 1) % dims[longest]
    return values.at[tuple(spot)].set(high)


def block_levels(stream_key, shape, split, low, high):
    gain, own = 1.0, jax.random.fold_in(stream_key, 6)
    for position, parts in split:
        draws = jnp.exp(jax.random.uniform(jax.random.fold_in(own, position), (parts,), jnp.float32, low / len(split), high / len(split)))
        gain = gain * jnp.repeat(draws, shape[position] // parts).reshape([-1 if axis == position else 1 for axis in range(len(shape))])
    return gain


def assign_block(own_key, own, number, rows, amount, top, limit, slope):
    order = jax.random.permutation(own_key, amount)
    packed, ordinary = load_shares(amount, rows * top, limit, slope, True), load_shares(amount, rows * top, limit, slope, False)
    places = jnp.arange(amount)

    def named(sizes, offset_by):
        used = int((sizes > 0).sum())
        fixed = max(1, used // 4)
        moved = fixed + (places - fixed + offset_by * (used - fixed)) % max(1, amount - fixed)
        return jnp.zeros((amount,), jnp.int32).at[order[jnp.where(places < fixed, places, moved)]].set(jnp.asarray(sizes, jnp.int32))

    sizes = jnp.where(number % 4 == 0, named(packed, number // 4), named(ordinary, number - number // 4 - 1))
    mixed = jax.random.permutation(jax.random.fold_in(own, 3), amount)
    source_of, receiver = mixed[0:amount // 2 * 2:2], mixed[1:amount // 2 * 2:2]
    margin = jnp.minimum(sizes[source_of] - 1, limit - sizes[receiver]) // 2
    margin = jnp.where((source_of == order[0]) | (receiver == order[0]) | (sizes[receiver] == 0), 0, jnp.maximum(margin, 0))
    moved = jax.random.randint(jax.random.fold_in(own, 4), (amount // 2,), 0, 1 << 20) % (margin + 1)
    sizes = sizes.at[source_of].add(-moved).at[receiver].add(moved)
    items = jnp.searchsorted(jnp.cumsum(sizes), jnp.arange(rows * top), side="right").astype(jnp.int32)
    grid = items.reshape(top, rows).T
    grid = grid[jax.random.permutation(jax.random.fold_in(own, 1), rows)]
    offset_by = jax.random.randint(jax.random.fold_in(own, 2), (rows, 1), 0, top)
    return jnp.take_along_axis(grid, (jnp.arange(top)[None, :] + offset_by) % top, axis=1)


def load_shares(number_of, total, bound, skew, full):
    portions = [(1 << 20) // math.isqrt(grade ** skew) + 1 for grade in range(1, number_of + 1)]
    largest = bound if full else min(bound, max(-(-total // number_of), total * portions[0] // sum(portions)))
    least = 1 if total - largest >= number_of - 1 else 0
    given, spare = [largest] + [least] * (number_of - 1), total - largest - least * (number_of - 1)
    while spare > 0:
        movable = [i for i in range(1, number_of) if given[i] < largest] or [i for i in range(1, number_of) if given[i] < bound]
        whole, budget = sum([portions[i] for i in movable]), spare
        for i in movable:
            extra = min(bound - given[i], max(1, budget * portions[i] // whole), spare)
            given[i] = given[i] + extra
            spare = spare - extra
    return np.array(given)


def centred(own_key, dims, spread, reach, split=(), kind=jnp.bfloat16):
    drawn = spread * jax.random.normal(own_key, dims, jnp.float32)
    if split:
        drawn = drawn * block_levels(own_key, dims, split, -0.22, 0.18)
    return jnp.clip(drawn, -reach, reach).astype(kind)


def setup_inputs(seed: int = 0) -> dict:
    arg_keys = jax.random.split(jax.random.key(seed), 9)
    fluid_offsets = jnp.clip(1.0 * jax.random.uniform(arg_keys[0], (3, NX, NY, NZ, 128), jnp.float32) ** block_levels(arg_keys[0], (3, NX, NY, NZ, 128), ((1, 2), (2, 4), (3, 4)), -0.2, 0.2), 0.0, 1.0)
    source = centred(arg_keys[1], (NX, NY, NZ, 128), 1.0, 6.0, ((0, 2), (1, 4), (2, 4)), jnp.float32)
    marker_offsets = jnp.clip(1.0 * jax.random.uniform(arg_keys[2], (GRAINS, MB, 3, 128), jnp.float32) ** block_levels(arg_keys[2], (GRAINS, MB, 3, 128), ((0, 32),), -0.2, 0.2), 0.0, 1.0)
    marker_normals = centred(arg_keys[3], (GRAINS, MB, 3, 128), 1.0, 6.0, ((0, 32),), jnp.float32)
    dest_tile_keys = jax.random.split(jax.random.fold_in(arg_keys[4], 1), GRAINS * MB // (G_DEV * MB))
    dest_tile_turns = jax.random.permutation(jax.random.fold_in(arg_keys[4], 3), GRAINS * MB // (G_DEV * MB))
    dest_tile = jax.vmap(lambda own, number: assign_block(jax.random.fold_in(arg_keys[4], 2), own, number, G_DEV * MB, N_FLOW * N_CROSS, 1, CAP, 2))(dest_tile_keys, dest_tile_turns).reshape((GRAINS, MB, 1))
    cell_index = touch_ends(jax.random.randint(arg_keys[5], (GRAINS, MB), 0, CELLS), jax.random.fold_in(arg_keys[5], 1), 0, CELLS - 1).astype(jnp.int32)
    grain_velocity = centred(arg_keys[6], (GRAINS, 3), 1.0, 6.0, ((0, 32),), jnp.float32)
    grain_mass = jnp.clip(jnp.exp(math.log(4.0) - 2.0794415 * jax.random.uniform(arg_keys[7], (GRAINS,), jnp.float32) ** block_levels(arg_keys[7], (GRAINS,), ((0, 32),), -0.2, 0.2)), 0.5, 4.0)
    return {"fluid_offsets": fluid_offsets, "source": source, "marker_offsets": marker_offsets, "marker_normals": marker_normals, "dest_tile": dest_tile, "cell_index": cell_index, "grain_velocity": grain_velocity, "grain_mass": grain_mass}


NEIGHBOURS = ((0, 0, 0), (1, 0, 0), (-1, 0, 0), (0, 1, 0), (0, -1, 0), (0, 0, 1), (0, 0, -1))
STIFFEN = 0.5
STEP_TIME = 0.05
PER_PARTICLE = 1.0 / 128.0


def pair_kernel(own_off, near_off, offset, values):
    total = None
    for component in range(3):
        gap = (near_off[component] + float(offset[component]))[..., None, :] - own_off[component][..., :, None]
        total = gap * gap if total is None else total + gap * gap
    weight = jnp.exp(-total) * PER_PARTICLE
    return jnp.sum(weight * values[..., None, :], axis=-1)


def marker_weights(fluid_rows, positions):
    total = None
    for component in range(3):
        gap = fluid_rows[:, component, :, None] - positions[:, component, None, :]
        total = gap * gap if total is None else total + gap * gap
    return jnp.exp(-total) * PER_PARTICLE


def weighted(fluid_offsets, field):
    def one_slab(slab_index):
        own_off = lax.dynamic_index_in_dim(fluid_offsets, slab_index, 1, keepdims=False)
        total = jnp.zeros(field.shape[1:], jnp.float32)
        for offset in NEIGHBOURS:
            near_index = (slab_index + offset[0]) % NX
            near_off = lax.dynamic_index_in_dim(fluid_offsets, near_index, 1, keepdims=False)
            near_val = lax.dynamic_index_in_dim(field, near_index, 0, keepdims=False)
            near_off = jnp.roll(near_off, (-offset[1], -offset[2]), axis=(1, 2))
            near_val = jnp.roll(near_val, (-offset[1], -offset[2]), axis=(0, 1))
            total = total + pair_kernel(own_off, near_off, offset, near_val)
        return total
    return lax.map(one_slab, jnp.arange(NX, dtype=jnp.int32))


def reference(fluid_offsets, source, marker_offsets, marker_normals, dest_tile, cell_index, grain_velocity, grain_mass):
    cell_count = NX * NY * NZ
    rowsum = weighted(fluid_offsets, jnp.ones(source.shape, jnp.float32))
    diagonal = STIFFEN + rowsum - PER_PARTICLE

    def operate(field):
        return (STIFFEN + rowsum) * field - weighted(fluid_offsets, field)

    fluid_rows = jnp.transpose(fluid_offsets, (1, 2, 3, 0, 4)).reshape(cell_count, 3, 128)
    device_count = N_FLOW * N_CROSS * N_DEPTH
    per_device = G_DEV * MB
    grain_ids = jnp.arange(GRAINS, dtype=jnp.int32)
    depth_of = (grain_ids // G_DEV) % N_DEPTH
    tile_of = dest_tile[:, :, 0]
    flow_of = tile_of // N_CROSS
    cross_of = tile_of % N_CROSS
    local_x = cell_index // (CY * CZ)
    local_y = (cell_index // CZ) % CY
    local_z = cell_index % CZ
    global_x = flow_of * CX + local_x
    global_y = cross_of * CY + local_y
    global_z = depth_of[:, None] * CZ + local_z
    target = ((global_x * NY + global_y) * NZ + global_z).astype(jnp.int32)
    target_groups = target.reshape(device_count, per_device)
    offset_groups = marker_offsets.reshape(device_count, per_device, 3, 128)
    normal_groups = marker_normals.reshape(device_count, per_device, 3, 128)

    velocity = grain_velocity
    displace = jnp.zeros(grain_velocity.shape, jnp.float32)
    pressure = jnp.zeros(source.shape, jnp.float32)
    for step_index in range(STEPS):
        moved = jnp.repeat(displace, MB, axis=0).reshape(device_count, per_device, 3)
        speeds = jnp.repeat(velocity, MB, axis=0).reshape(device_count, per_device, 3)

        def contribute(pieces):
            targets, offsets, normals, shifted, moving = pieces
            positions = offsets + shifted[:, :, None]
            rate = normals[:, 0] * moving[:, 0, None] + normals[:, 1] * moving[:, 1, None] + normals[:, 2] * moving[:, 2, None]
            weight = marker_weights(fluid_rows[targets], positions)
            return jnp.sum(weight * rate[:, None, :], axis=-1)

        added = lax.map(contribute, (target_groups, offset_groups, normal_groups, moved, speeds))
        summed = jnp.zeros((cell_count, 128), jnp.float32).at[target.reshape(-1)].add(added.reshape(-1, 128))
        right_side = source + summed.reshape(source.shape)

        solution = pressure
        residual = right_side - operate(solution)
        precond = residual / diagonal
        direction = precond
        norm_now = jnp.sum(residual * precond)
        for iteration in range(ITERS):
            image = operate(direction)
            alpha = norm_now / jnp.sum(direction * image)
            solution = solution + alpha * direction
            residual = residual - alpha * image
            precond = residual / diagonal
            norm_next = jnp.sum(residual * precond)
            direction = precond + (norm_next / norm_now) * direction
            norm_now = norm_next
        pressure = solution
        pressure_rows = pressure.reshape(cell_count, 128)

        def push(pieces):
            targets, offsets, normals, shifted = pieces
            positions = offsets + shifted[:, :, None]
            weight = marker_weights(fluid_rows[targets], positions)
            felt = jnp.sum(weight * pressure_rows[targets][:, :, None], axis=1)
            return jnp.sum(normals * felt[:, None, :], axis=-1)

        block_force = lax.map(push, (target_groups, offset_groups, normal_groups, moved)).reshape(GRAINS, MB, 3)
        grain_force = jnp.sum(block_force, axis=1)
        velocity = velocity + STEP_TIME * grain_force / grain_mass[:, None]
        displace = displace + STEP_TIME * velocity
    return pressure, velocity
```

```python
import functools
import math

import jax
import jax.numpy as jnp
from jax import lax
from jax.experimental import pallas as pl
from jax.experimental.pallas import tpu as pltpu
from jax.sharding import PartitionSpec as P

ITERS = 4
STEPS = 2
STIFFEN = 0.5
STEP_TIME = 0.05
PER_PARTICLE = 1.0 / 128.0
SCALE = math.sqrt(math.log2(math.e))
SHIFT = math.log2(PER_PARTICLE)
MESH = pl.DeviceIdType.MESH
ROWS = 8
GROUP = 4
MIDDLE = 0.5


def weight_of(gaps):
    total = None
    for gap in gaps:
        total = gap * gap if total is None else total + gap * gap
    return jnp.exp2(SHIFT - total)


def rounded(value):
    return value.astype(jnp.bfloat16).astype(jnp.float32)


def solve_small(gram, right):
    n = len(right)
    gram = [list(row) for row in gram]
    right = list(right)
    for i in range(n):
        inverse = 1.0 / gram[i][i]
        for j in range(i + 1, n):
            factor = gram[j][i] * inverse
            for k in range(i + 1, n):
                gram[j][k] = gram[j][k] - factor * gram[i][k]
            right[j] = right[j] - factor * right[i]
    out = [None] * n
    for i in reversed(range(n)):
        value = right[i]
        for k in range(i + 1, n):
            value = value - gram[i][k] * out[k]
        out[i] = value / gram[i][i]
    return out


def two_parts(value):
    high = rounded(value)
    return high, value - high


def kernel(
    sizes,
    dims,
    off_ref,
    source_ref,
    points_ref,
    normals_ref,
    tile_ref,
    cell_ref,
    start_ref,
    mass_ref,
    press_out,
    speed_out,
    off_group,
    off_depth,
    weights,
    own_rows,
    own_columns,
    point_rows,
    point_parts,
    normal_rows,
    normal_parts,
    near,
    normal_sums,
    added,
    felt_rows,
    speed_rows,
    mass_rows,
    moved_rows,
    own_shift,
    point_shift,
    place_rows,
    place_ref,
    give,
    take,
    krylov,
    krylov_depth,
    part_group,
    part_depth,
    off_send,
    off_recv,
    take_send,
    take_recv,
    kry_send,
    kry_recv,
    part_send,
    part_recv,
    place_sem,
):
    n_flow, n_cross, n_depth = sizes
    size_x, size_y, size_z = dims
    cells = size_x * size_y * size_z
    tiles = n_flow * n_cross
    grains, _, per_grain, lanes = points_ref.shape
    blocks = grains * per_grain
    flow, cross, depth = (lax.axis_index("flow"), lax.axis_index("cross"), lax.axis_index("depth"))

    def group_at(slot):
        rf, rc = divmod(slot, n_cross)
        return (lax.rem(flow + rf, n_flow), lax.rem(cross + rc, n_cross), depth)

    def group_back(slot):
        rf, rc = divmod(slot, n_cross)
        return (
            lax.rem(flow + n_flow - rf, n_flow),
            lax.rem(cross + n_cross - rc, n_cross),
            depth,
        )

    def depth_at(rd):
        return (flow, cross, lax.rem(depth + rd, n_depth))

    slot_flow = {1: (n_flow - 1) * n_cross, -1: (1 % n_flow) * n_cross}
    slot_cross = {1: n_cross - 1, -1: 1 % n_cross}
    near_slots = sorted({slot_flow[1], slot_flow[-1], slot_cross[1], slot_cross[-1]} - {0})
    far_slots = [r for r in range(1, tiles) if r not in near_slots]
    near_slots = sorted(near_slots, key=lambda r: r // n_cross)
    order = near_slots + far_slots
    near_depth = sorted({1, n_depth - 1})
    depth_index = {1: near_depth.index(n_depth - 1), -1: near_depth.index(1)}

    barrier = pltpu.get_barrier_semaphore()
    for r in range(1, tiles):
        pl.semaphore_signal(barrier, inc=1, device_id=group_at(r), device_id_type=MESH)
    for rd in range(1, n_depth):
        pl.semaphore_signal(barrier, inc=1, device_id=depth_at(rd), device_id_type=MESH)

    row = lax.broadcasted_iota(jnp.int32, (ROWS, lanes), 0)

    tile = tile_ref[:, 0, :]
    slot_flow_of = lax.rem(flow + n_flow - lax.div(tile, n_cross), n_flow)
    slot_cross_of = lax.rem(cross + n_cross - lax.rem(tile, n_cross), n_cross)
    slot_of = slot_flow_of * n_cross + slot_cross_of
    place_rows[...] = jnp.zeros(place_rows.shape, jnp.int32)
    place_rows[:, :per_grain] = slot_of * cells + cell_ref[...]
    place_copy = pltpu.make_async_copy(place_rows, place_ref, place_sem)
    place_copy.start()

    spot = lax.broadcasted_iota(jnp.int32, (per_grain, blocks), 1)
    pick = (
        lax.rem(spot, per_grain) == lax.broadcasted_iota(jnp.int32, (per_grain, blocks), 0)
    ).astype(jnp.bfloat16)
    held = (
        lax.div(lax.broadcasted_iota(jnp.int32, (grains, blocks), 1), per_grain)
        == lax.broadcasted_iota(jnp.int32, (grains, blocks), 0)
    )

    def in_a_row(value):
        spread = jnp.dot(
            value.astype(jnp.float32).astype(jnp.bfloat16),
            pick,
            preferred_element_type=jnp.float32,
        )
        return jnp.sum(jnp.where(held, spread, 0.0), axis=0, keepdims=True)

    place_row = in_a_row(slot_of) * cells + in_a_row(cell_ref[...])
    one_hot = jnp.where(
        lax.broadcasted_iota(jnp.int32, (tiles * cells, blocks), 0).astype(jnp.float32)
        == place_row,
        1.0,
        0.0,
    ).astype(jnp.bfloat16)

    def prepare(g, carry):
        for b in range(per_grain):
            point = jnp.where(row > 3, 1.0, 0.0)
            normal = jnp.zeros((ROWS, lanes), jnp.float32)
            for c in range(3):
                point = jnp.where(
                    row == c, SCALE * (points_ref[g, c, b : b + 1, :] - MIDDLE), point
                )
                normal = jnp.where(row == c, normals_ref[g, c, b : b + 1, :], normal)
            square = jnp.sum(jnp.where(row < 3, point * point, 0.0), axis=0, keepdims=True)
            point = jnp.where(row == 3, square, point)
            point_rows[g, b] = point
            point_parts[g, b] = jnp.concatenate(two_parts(point), axis=0).astype(jnp.bfloat16)
            normal_rows[g, b] = normal
            normal_parts[g, b] = jnp.concatenate(two_parts(normal), axis=0).astype(jnp.bfloat16)
        return carry

    lax.fori_loop(0, grains, prepare, 0)
    place_copy.wait()
    pl.semaphore_wait(barrier, tiles - 1 + n_depth - 1)

    sent = []

    def ship(src, dst, send_sem, recv_sem, device):
        copy = pltpu.make_async_remote_copy(
            src_ref=src,
            dst_ref=dst,
            send_sem=send_sem,
            recv_sem=recv_sem,
            device_id=device,
            device_id_type=MESH,
        )
        copy.start()
        sent.append(copy)
        return copy

    off_copies = {}
    for r in order:
        off_copies[r] = ship(
            off_ref, off_group.at[r], off_send.at[r], off_recv.at[r], group_at(r)
        )
    off_depth_copies = []
    for i, rd in enumerate(near_depth):
        off_depth_copies.append(
            ship(
                off_ref,
                off_depth.at[i],
                off_send.at[tiles + i],
                off_recv.at[tiles + i],
                depth_at(rd),
            )
        )
    off_group[0] = off_ref[...]

    def own_pass(slot, carry):
        for low in range(0, cells, GROUP):
            stacked = []
            for cell in range(low, low + GROUP):
                base = jnp.where(row == 3, -1.0, jnp.where(row == 5, SHIFT, 0.0))
                square = None
                for c in range(3):
                    spot = c * cells + cell
                    own = SCALE * (off_group[slot, spot : spot + 1, :] - MIDDLE)
                    base = jnp.where(row == c, 2.0 * own, base)
                    square = own * own if square is None else square + own * own
                base = jnp.where(row == 4, -square, base)
                own_rows[slot * cells + cell] = base
                high, rest = two_parts(base)
                stacked += [high, high, rest, rest]
            own_columns[slot * (cells // GROUP) + low // GROUP] = jnp.transpose(
                jnp.concatenate(stacked, axis=0)
            ).astype(jnp.bfloat16)
        return carry

    for r in order:
        off_copies[r].wait_recv()
    lax.fori_loop(0, tiles, own_pass, 0)

    def near_pass(g, carry):
        for b in range(per_grain):
            place = place_ref[g, b]
            member = lax.rem(place, GROUP)
            parts = point_parts[g, b]
            stacked = []
            for k in range(GROUP):
                picked = jnp.where(member == k, parts, jnp.zeros_like(parts))
                stacked += [picked, picked]
            weight = jnp.exp2(
                jnp.dot(
                    own_columns[lax.div(place, GROUP)],
                    jnp.concatenate(stacked, axis=0),
                    preferred_element_type=jnp.float32,
                )
            )
            upper = weight.astype(jnp.bfloat16)
            near[g * per_grain + b, :, :lanes] = upper
            near[g * per_grain + b, :, lanes:] = (weight - upper.astype(jnp.float32)).astype(
                jnp.bfloat16
            )
        return carry

    lax.fori_loop(0, grains, near_pass, 0)

    def weigh(step, velocity, own_shift, point_shift):
        def body(g, carry):
            rows = []
            half = lax.broadcasted_iota(jnp.int32, (per_grain, lanes), 0)
            rates = jnp.zeros((per_grain, lanes), jnp.float32)
            for b in range(per_grain):
                if step:
                    factor = jnp.exp2(
                        jnp.sum(point_rows[g, b] * point_shift[g], axis=0, keepdims=True)
                    )
                    parts = jnp.concatenate(
                        two_parts(normal_rows[g, b] * factor), axis=0
                    ).astype(jnp.bfloat16)
                else:
                    parts = normal_parts[g, b]
                total = lax.dot_general(
                    jnp.concatenate([parts, parts], axis=1),
                    near[g * per_grain + b],
                    (((1,), (1,)), ((), ())),
                    preferred_element_type=jnp.float32,
                )
                total = total[:ROWS] + total[ROWS:]
                if step:
                    factor = jnp.exp2(
                        jnp.sum(
                            own_rows[place_ref[g, b]] * own_shift[g], axis=0, keepdims=True
                        )
                    )
                    total = total * factor
                normal_sums[g, b] = total
                rate = jnp.sum(total * velocity[g], axis=0, keepdims=True)
                rates = jnp.where(half == b, rate, rates)
            added[pl.ds(pl.multiple_of(g * per_grain, ROWS), per_grain), :] = rates
            return carry

        lax.fori_loop(0, grains, body, 0)

    def to_fluid(step):
        high, rest = two_parts(added[...])
        spread = jnp.dot(
            one_hot,
            jnp.concatenate([high, rest], axis=1).astype(jnp.bfloat16),
            preferred_element_type=jnp.float32,
        )
        spread = spread[:, :lanes] + spread[:, lanes:]
        give[step] = spread.reshape(tiles, cells, lanes)
        return [
            ship(
                give.at[step, r],
                take.at[step, r],
                take_send.at[step, r],
                take_recv.at[step, r],
                group_back(r),
            )
            for r in reversed(order)
        ]

    def collect(step, copies):
        total = give[step, 0]
        for copy in copies:
            copy.wait_recv()
        for r in range(1, tiles):
            total = total + take[step, r]
        return total

    merged = size_x == 1 and n_flow == 2
    sources = {("own", 0): 0}
    flow_keys = [("flow", 1)] if merged else [("flow", 1), ("flow", -1)]
    for key in flow_keys + [("cross", 1), ("cross", -1), ("depth", 1), ("depth", -1)]:
        sources[key] = len(sources)
    padded_rows = -(-len(sources) * cells // 128) * 128

    def columns_of(pick):
        rows = []
        for axis, side in sources:
            if axis == "own":
                rows.append(pick(0, None))
            elif axis == "flow":
                rows.append(pick(slot_flow[side], None))
            elif axis == "cross":
                rows.append(pick(slot_cross[side], None))
            else:
                rows.append(pick(None, depth_index[side]))
        spare = padded_rows - len(sources) * cells
        if spare:
            rows.append(jnp.zeros((spare, lanes), jnp.float32))
        return jnp.transpose(jnp.concatenate(rows, axis=0))

    def pairs(cell):
        x, rest = divmod(cell, size_y * size_z)
        y, z = divmod(rest, size_z)
        found = [(cell, (0, 0, 0))]
        place, extent, names = (x, y, z), (size_x, size_y, size_z), ("flow", "cross", "depth")
        for axis in range(3):
            for side in (1, -1):
                near = list(place)
                near[axis] += side
                key = ("own", 0)
                if not 0 <= near[axis] < extent[axis]:
                    near[axis] %= extent[axis]
                    key = (names[axis], side)
                    if axis == 0 and merged:
                        key = (names[axis], 1)
                index = (near[0] * size_y + near[1]) * size_z + near[2]
                step = [0, 0, 0]
                step[axis] = side
                found.append((sources[key] * cells + index, tuple(step)))
        return found

    groups = []
    for cell in range(cells):
        by_column = {}
        for column, step in pairs(cell):
            by_column.setdefault(column, []).append(step)
        groups.append(list(by_column.items()))

    start = jnp.zeros((ROWS, grains), jnp.float32)
    grain_row = lax.broadcasted_iota(jnp.int32, (ROWS, grains), 0)
    for c in range(3):
        start = jnp.where(grain_row == c, start_ref[c : c + 1, :], start)
    for g in range(grains):
        speed_rows[g] = jnp.broadcast_to(start[:, g : g + 1], (ROWS, lanes))
        mass_rows[g] = jnp.broadcast_to(mass_ref[:, g : g + 1], (ROWS, lanes))
        moved_rows[g] = jnp.zeros((ROWS, lanes), jnp.float32)

    weigh(0, speed_rows, None, None)
    copies = to_fluid(0)
    for copy in off_depth_copies:
        copy.wait_recv()

    turned = [
        SCALE
        * columns_of(
            lambda slot, i, c=c: (
                off_group[slot, c * cells : (c + 1) * cells, :]
                if i is None
                else off_depth[i, c * cells : (c + 1) * cells, :]
            )
        )
        for c in range(3)
    ]
    sum_rows = []
    for cell in range(cells):
        own = [
            SCALE * off_ref[c * cells + cell : c * cells + cell + 1, :] for c in range(3)
        ]
        full = None
        for position, (column, steps) in enumerate(groups[cell]):
            total = None
            for step in steps:
                weight = weight_of(
                    [
                        turned[c][:, column : column + 1] - (own[c] - SCALE * step[c])
                        for c in range(3)
                    ]
                )
                total = weight if total is None else total + weight
            weights[cell, position] = total
            full = total if full is None else full + total
        sum_rows.append(jnp.sum(full, axis=0, keepdims=True))
    rowsum = jnp.concatenate(sum_rows, axis=0)
    diagonal = STIFFEN + rowsum - PER_PARTICLE
    inverse = 1.0 / diagonal

    def weighted(step, j):
        turned_field = columns_of(
            lambda slot, i: krylov[step, j, slot] if i is None else krylov_depth[step, j, i]
        )
        rows = []
        for cell in range(cells):
            total = None
            for low in range(0, lanes, 64):
                acc = None
                for position, (column, _) in enumerate(groups[cell]):
                    term = (
                        weights[cell, position, low : low + 64, :]
                        * turned_field[low : low + 64, column : column + 1]
                    )
                    acc = term if acc is None else acc + term
                acc = jnp.sum(acc.reshape(8, 8, lanes), axis=0)
                total = acc if total is None else total + acc
            rows.append(jnp.sum(total, axis=0, keepdims=True))
        return jnp.concatenate(rows, axis=0)

    pressure = jnp.zeros((cells, lanes), jnp.float32)
    spread_before = None
    residual = None
    pressure_all = None
    for step in range(STEPS):
        if step:
            for g in range(grains):
                shift = SCALE * moved_rows[g]
                square = 0.5 * jnp.sum(shift * shift, axis=0, keepdims=True)
                own_shift[g] = jnp.where(row == 3, square, shift)
                point_shift[g] = jnp.where(row == 4, -square, -2.0 * shift)
            weigh(step, speed_rows, own_shift, point_shift)
            copies = to_fluid(step)
        spread = collect(step, copies)
        if step == 0:
            residual = source_ref[...] + spread
        else:
            residual = residual + (spread - spread_before)
        spread_before = spread
        fields = [residual * inverse]
        far = []
        for j in range(ITERS):
            krylov[step, j, 0] = fields[j]
            close = {}
            for r in near_slots:
                close[r] = ship(
                    krylov.at[step, j, 0],
                    krylov.at[step, j, r],
                    kry_send.at[step, j, r],
                    kry_recv.at[step, j, r],
                    group_at(r),
                )
            beside = [
                ship(
                    krylov.at[step, j, 0],
                    krylov_depth.at[step, j, i],
                    kry_send.at[step, j, tiles + i],
                    kry_recv.at[step, j, tiles + i],
                    depth_at(rd),
                )
                for i, rd in enumerate(near_depth)
            ]
            for r in far_slots:
                far.append(
                    ship(
                        krylov.at[step, j, 0],
                        krylov.at[step, j, r],
                        kry_send.at[step, j, r],
                        kry_recv.at[step, j, r],
                        group_at(r),
                    )
                )
            for copy in list(close.values()) + beside:
                copy.wait_recv()
            fields.append((weighted(step, j) - PER_PARTICLE * fields[j]) * inverse)
        moments = []
        for j in range(ITERS):
            scaled = diagonal * fields[j]
            moments.append(jnp.sum(scaled * fields[j], axis=0, keepdims=True))
            moments.append(jnp.sum(scaled * fields[j + 1], axis=0, keepdims=True))
        part_group[step, 0] = jnp.concatenate(moments, axis=0)
        waits = [
            ship(
                part_group.at[step, 0],
                part_group.at[step, r],
                part_send.at[step, r],
                part_recv.at[step, r],
                group_at(r),
            )
            for r in order
        ]
        for copy in waits:
            copy.wait_recv()
        total = part_group[step, 0]
        for r in range(1, tiles):
            total = total + part_group[step, r]
        part_depth[step, 0] = total
        waits = [
            ship(
                part_depth.at[step, 0],
                part_depth.at[step, rd],
                part_send.at[step, tiles + rd],
                part_recv.at[step, tiles + rd],
                depth_at(rd),
            )
            for rd in range(1, n_depth)
        ]
        for copy in waits:
            copy.wait_recv()
        for rd in range(1, n_depth):
            total = total + part_depth[step, rd]
        total = jnp.broadcast_to(jnp.sum(total, axis=1, keepdims=True), total.shape)
        scalars = [total[q : q + 1, :] for q in range(2 * ITERS)]
        gram = [
            [scalars[i + j] - scalars[i + j + 1] for j in range(ITERS)] for i in range(ITERS)
        ]
        factors = solve_small(gram, scalars[:ITERS])
        for j in range(ITERS):
            pressure = pressure + factors[j] * fields[j]
            residual = residual - factors[j] * (diagonal * (fields[j] - fields[j + 1]))
        for copy in far:
            copy.wait_recv()
        for j in range(ITERS):
            term = factors[j] * krylov[step, j].reshape(tiles * cells, lanes)
            pressure_all = term if pressure_all is None else pressure_all + term
        felt_rows[...] = pressure_all

        def push(g, carry):
            total = None
            for b in range(per_grain):
                felt = felt_rows[pl.ds(place_ref[g, b], 1), :]
                term = normal_sums[g, b] * felt
                total = term if total is None else total + term
            force = jnp.broadcast_to(
                jnp.sum(total, axis=1, keepdims=True), (ROWS, lanes)
            )
            speed = speed_rows[g] + STEP_TIME * force / mass_rows[g]
            speed_rows[g] = speed
            moved_rows[g] = moved_rows[g] + STEP_TIME * speed
            return carry

        lax.fori_loop(0, grains, push, 0)
    press_out[...] = pressure
    lane = lax.broadcasted_iota(jnp.int32, (ROWS, lanes), 1)
    speed = jnp.zeros((ROWS, lanes), jnp.float32)
    for g in range(grains):
        speed = jnp.where(lane == g, speed_rows[g], speed)
    speed_out[...] = speed[:3, :grains]
    for copy in sent:
        copy.wait_send()


def per_device(
    sizes,
    fluid_offsets,
    source,
    marker_offsets,
    marker_normals,
    dest_tile,
    cell_index,
    grain_velocity,
    grain_mass,
):
    n_flow, n_cross, n_depth = sizes
    tiles = n_flow * n_cross
    dims = source.shape[:3]
    cells = dims[0] * dims[1] * dims[2]
    lanes = source.shape[3]
    grains, per_grain = cell_index.shape
    blocks = grains * per_grain
    near_count = len({1, n_depth - 1})
    vmem, dma = pltpu.VMEM, pltpu.SemaphoreType.DMA
    f32 = jnp.float32
    in_vmem = pl.BlockSpec(memory_space=pltpu.VMEM)
    pressure, speed = pl.pallas_call(
        functools.partial(kernel, sizes, dims),
        out_shape=(
            jax.ShapeDtypeStruct((cells, lanes), f32),
            jax.ShapeDtypeStruct((3, grains), f32),
        ),
        in_specs=[in_vmem] * 8,
        out_specs=(in_vmem, in_vmem),
        scratch_shapes=[
            vmem((tiles, 3 * cells, lanes), f32),
            vmem((near_count, 3 * cells, lanes), f32),
            vmem((cells, 7, lanes, lanes), f32),
            vmem((tiles * cells, ROWS, lanes), f32),
            vmem((tiles * cells // GROUP, lanes, 4 * ROWS * GROUP), jnp.bfloat16),
            vmem((grains, per_grain, ROWS, lanes), f32),
            vmem((grains, per_grain, 2 * ROWS, lanes), jnp.bfloat16),
            vmem((grains, per_grain, ROWS, lanes), f32),
            vmem((grains, per_grain, 2 * ROWS, lanes), jnp.bfloat16),
            vmem((blocks, lanes, 2 * lanes), jnp.bfloat16),
            vmem((grains, per_grain, ROWS, lanes), f32),
            vmem((blocks, lanes), f32),
            vmem((tiles * cells, lanes), f32),
            vmem((grains, ROWS, lanes), f32),
            vmem((grains, ROWS, lanes), f32),
            vmem((grains, ROWS, lanes), f32),
            vmem((grains, ROWS, lanes), f32),
            vmem((grains, ROWS, lanes), f32),
            vmem((grains, lanes), jnp.int32),
            pltpu.SMEM((grains, lanes), jnp.int32),
            vmem((STEPS, tiles, cells, lanes), f32),
            vmem((STEPS, tiles, cells, lanes), f32),
            vmem((STEPS, ITERS, tiles, cells, lanes), f32),
            vmem((STEPS, ITERS, near_count, cells, lanes), f32),
            vmem((STEPS, tiles, 2 * ITERS, lanes), f32),
            vmem((STEPS, n_depth, 2 * ITERS, lanes), f32),
            dma((tiles + near_count,)),
            dma((tiles + near_count,)),
            dma((STEPS, tiles)),
            dma((STEPS, tiles)),
            dma((STEPS, ITERS, tiles + near_count)),
            dma((STEPS, ITERS, tiles + near_count)),
            dma((STEPS, tiles + n_depth)),
            dma((STEPS, tiles + n_depth)),
            dma,
        ],
        compiler_params=pltpu.CompilerParams(
            collective_id=0, has_side_effects=True, vmem_limit_bytes=60 * 1024 * 1024
        ),
        name="coupled",
    )(
        fluid_offsets.reshape(3 * cells, lanes),
        source.reshape(cells, lanes),
        jnp.transpose(marker_offsets, (0, 2, 1, 3)),
        jnp.transpose(marker_normals, (0, 2, 1, 3)),
        jnp.transpose(dest_tile, (0, 2, 1)),
        cell_index,
        jnp.transpose(grain_velocity),
        grain_mass[None, :],
    )
    return (pressure.reshape(source.shape), jnp.transpose(speed))


def solution(mesh):
    sizes = tuple(mesh.shape[name] for name in ("flow", "cross", "depth"))
    return jax.shard_map(
        functools.partial(per_device, sizes),
        mesh=mesh,
        in_specs=(
            P(None, "flow", "cross", "depth", None),
            P("flow", "cross", "depth", None),
            P(("flow", "cross", "depth"), None, None, None),
            P(("flow", "cross", "depth"), None, None, None),
            P(("flow", "cross", "depth"), None, None),
            P(("flow", "cross", "depth"), None),
            P(("flow", "cross", "depth"), None),
            P(("flow", "cross", "depth")),
        ),
        out_specs=(P("flow", "cross", "depth", None), P(("flow", "cross", "depth"), None)),
        check_vma=False,
    )
```

```python
import functools
import math

import jax
import jax.numpy as jnp
from jax import lax
from jax.experimental import pallas as pl
from jax.experimental.pallas import tpu as pltpu
from jax.sharding import PartitionSpec as P

ITERS = 4
STEPS = 2
STIFFEN = 0.5
STEP_TIME = 0.05
PER_PARTICLE = 1.0 / 128.0
SCALE = math.sqrt(math.log2(math.e))
SHIFT = math.log2(PER_PARTICLE)
MESH = pl.DeviceIdType.MESH
ROWS = 8
GROUP = 4
MIDDLE = 0.5


def weight_of(gaps):
    total = None
    for gap in gaps:
        total = gap * gap if total is None else total + gap * gap
    return jnp.exp2(SHIFT - total)


def rounded(value):
    return value.astype(jnp.bfloat16).astype(jnp.float32)


def solve_small(gram, right):
    n = len(right)
    gram = [list(row) for row in gram]
    right = list(right)
    for i in range(n):
        inverse = 1.0 / gram[i][i]
        for j in range(i + 1, n):
            factor = gram[j][i] * inverse
            for k in range(i + 1, n):
                gram[j][k] = gram[j][k] - factor * gram[i][k]
            right[j] = right[j] - factor * right[i]
    out = [None] * n
    for i in reversed(range(n)):
        value = right[i]
        for k in range(i + 1, n):
            value = value - gram[i][k] * out[k]
        out[i] = value / gram[i][i]
    return out


def two_parts(value):
    high = rounded(value)
    return high, value - high


def kernel(
    sizes,
    dims,
    off_ref,
    source_ref,
    points_ref,
    normals_ref,
    tile_ref,
    cell_ref,
    start_ref,
    mass_ref,
    press_out,
    speed_out,
    off_group,
    off_depth,
    weights,
    own_rows,
    own_columns,
    point_rows,
    point_parts,
    normal_rows,
    normal_parts,
    near,
    normal_sums,
    added,
    felt_rows,
    speed_rows,
    mass_rows,
    moved_rows,
    own_shift,
    point_shift,
    place_rows,
    place_ref,
    give,
    take,
    krylov,
    krylov_depth,
    part,
    off_send,
    off_recv,
    take_send,
    take_recv,
    kry_send,
    kry_recv,
    part_send,
    part_recv,
    place_sem,
):
    n_flow, n_cross, n_depth = sizes
    size_x, size_y, size_z = dims
    cells = size_x * size_y * size_z
    tiles = n_flow * n_cross
    grains, _, per_grain, lanes = points_ref.shape
    blocks = grains * per_grain
    flow, cross, depth = (lax.axis_index("flow"), lax.axis_index("cross"), lax.axis_index("depth"))

    def group_at(slot):
        rf, rc = divmod(slot, n_cross)
        return (lax.rem(flow + rf, n_flow), lax.rem(cross + rc, n_cross), depth)

    def group_back(slot):
        rf, rc = divmod(slot, n_cross)
        return (
            lax.rem(flow + n_flow - rf, n_flow),
            lax.rem(cross + n_cross - rc, n_cross),
            depth,
        )

    def depth_at(rd):
        return (flow, cross, lax.rem(depth + rd, n_depth))

    slot_flow = {1: (n_flow - 1) * n_cross, -1: (1 % n_flow) * n_cross}
    slot_cross = {1: n_cross - 1, -1: 1 % n_cross}
    near_slots = sorted({slot_flow[1], slot_flow[-1], slot_cross[1], slot_cross[-1]} - {0})
    far_slots = [r for r in range(1, tiles) if r not in near_slots]
    near_slots = sorted(near_slots, key=lambda r: r // n_cross)
    order = near_slots + far_slots
    near_depth = sorted({1, n_depth - 1})
    depth_index = {1: near_depth.index(n_depth - 1), -1: near_depth.index(1)}

    barrier = pltpu.get_barrier_semaphore()
    def everyone_at(r, rd):
        there = group_at(r)
        return (there[0], there[1], lax.rem(depth + rd, n_depth))

    everyone = [(r, rd) for r in [0] + order for rd in range(n_depth) if (r, rd) != (0, 0)]
    everyone = everyone[::-1]
    for r, rd in everyone:
        pl.semaphore_signal(barrier, inc=1, device_id=everyone_at(r, rd), device_id_type=MESH)

    row = lax.broadcasted_iota(jnp.int32, (ROWS, lanes), 0)

    tile = tile_ref[:, 0, :]
    slot_flow_of = lax.rem(flow + n_flow - lax.div(tile, n_cross), n_flow)
    slot_cross_of = lax.rem(cross + n_cross - lax.rem(tile, n_cross), n_cross)
    slot_of = slot_flow_of * n_cross + slot_cross_of
    place_rows[...] = jnp.zeros(place_rows.shape, jnp.int32)
    place_rows[:, :per_grain] = slot_of * cells + cell_ref[...]
    place_copy = pltpu.make_async_copy(place_rows, place_ref, place_sem)
    place_copy.start()

    spot = lax.broadcasted_iota(jnp.int32, (per_grain, blocks), 1)
    pick = (
        lax.rem(spot, per_grain) == lax.broadcasted_iota(jnp.int32, (per_grain, blocks), 0)
    ).astype(jnp.bfloat16)
    held = (
        lax.div(lax.broadcasted_iota(jnp.int32, (grains, blocks), 1), per_grain)
        == lax.broadcasted_iota(jnp.int32, (grains, blocks), 0)
    )

    def in_a_row(value):
        spread = jnp.dot(
            value.astype(jnp.float32).astype(jnp.bfloat16),
            pick,
            preferred_element_type=jnp.float32,
        )
        return jnp.sum(jnp.where(held, spread, 0.0), axis=0, keepdims=True)

    place_row = in_a_row(slot_of) * cells + in_a_row(cell_ref[...])
    one_hot = jnp.where(
        lax.broadcasted_iota(jnp.int32, (tiles * cells, blocks), 0).astype(jnp.float32)
        == place_row,
        1.0,
        0.0,
    ).astype(jnp.bfloat16)

    def prepare(g, carry):
        for b in range(per_grain):
            point = jnp.where(row > 3, 1.0, 0.0)
            normal = jnp.zeros((ROWS, lanes), jnp.float32)
            for c in range(3):
                point = jnp.where(
                    row == c, SCALE * (points_ref[g, c, b : b + 1, :] - MIDDLE), point
                )
                normal = jnp.where(row == c, normals_ref[g, c, b : b + 1, :], normal)
            square = jnp.sum(jnp.where(row < 3, point * point, 0.0), axis=0, keepdims=True)
            point = jnp.where(row == 3, square, point)
            point_rows[g, b] = point
            point_parts[g, b] = jnp.concatenate(two_parts(point), axis=0).astype(jnp.bfloat16)
            normal_rows[g, b] = normal
            normal_parts[g, b] = jnp.concatenate(two_parts(normal), axis=0).astype(jnp.bfloat16)
        return carry

    lax.fori_loop(0, grains, prepare, 0)
    place_copy.wait()
    pl.semaphore_wait(barrier, len(everyone))

    sent = []

    def ship(src, dst, send_sem, recv_sem, device):
        copy = pltpu.make_async_remote_copy(
            src_ref=src,
            dst_ref=dst,
            send_sem=send_sem,
            recv_sem=recv_sem,
            device_id=device,
            device_id_type=MESH,
        )
        copy.start()
        sent.append(copy)
        return copy

    off_copies = {}
    for r in order:
        off_copies[r] = ship(
            off_ref, off_group.at[r], off_send.at[r], off_recv.at[r], group_at(r)
        )
    off_depth_copies = []
    for i, rd in enumerate(near_depth):
        off_depth_copies.append(
            ship(
                off_ref,
                off_depth.at[i],
                off_send.at[tiles + i],
                off_recv.at[tiles + i],
                depth_at(rd),
            )
        )
    off_group[0] = off_ref[...]

    def own_pass(slot, carry):
        for low in range(0, cells, GROUP):
            stacked = []
            for cell in range(low, low + GROUP):
                base = jnp.where(row == 3, -1.0, jnp.where(row == 5, SHIFT, 0.0))
                square = None
                for c in range(3):
                    spot = c * cells + cell
                    own = SCALE * (off_group[slot, spot : spot + 1, :] - MIDDLE)
                    base = jnp.where(row == c, 2.0 * own, base)
                    square = own * own if square is None else square + own * own
                base = jnp.where(row == 4, -square, base)
                own_rows[slot * cells + cell] = base
                high, rest = two_parts(base)
                stacked += [high, high, rest, rest]
            own_columns[slot * (cells // GROUP) + low // GROUP] = jnp.transpose(
                jnp.concatenate(stacked, axis=0)
            ).astype(jnp.bfloat16)
        return carry

    for r in order:
        off_copies[r].wait_recv()
    lax.fori_loop(0, tiles, own_pass, 0)

    def near_pass(g, carry):
        for b in range(per_grain):
            place = place_ref[g, b]
            member = lax.rem(place, GROUP)
            parts = point_parts[g, b]
            stacked = []
            for k in range(GROUP):
                picked = jnp.where(member == k, parts, jnp.zeros_like(parts))
                stacked += [picked, picked]
            weight = jnp.exp2(
                jnp.dot(
                    own_columns[lax.div(place, GROUP)],
                    jnp.concatenate(stacked, axis=0),
                    preferred_element_type=jnp.float32,
                )
            )
            upper = weight.astype(jnp.bfloat16)
            near[g * per_grain + b, :, :lanes] = upper
            near[g * per_grain + b, :, lanes:] = (weight - upper.astype(jnp.float32)).astype(
                jnp.bfloat16
            )
        return carry

    lax.fori_loop(0, grains, near_pass, 0)

    def weigh(step, velocity, own_shift, point_shift):
        def body(g, carry):
            rows = []
            half = lax.broadcasted_iota(jnp.int32, (per_grain, lanes), 0)
            rates = jnp.zeros((per_grain, lanes), jnp.float32)
            for b in range(per_grain):
                if step:
                    factor = jnp.exp2(
                        jnp.sum(point_rows[g, b] * point_shift[g], axis=0, keepdims=True)
                    )
                    parts = jnp.concatenate(
                        two_parts(normal_rows[g, b] * factor), axis=0
                    ).astype(jnp.bfloat16)
                else:
                    parts = normal_parts[g, b]
                total = lax.dot_general(
                    jnp.concatenate([parts, parts], axis=1),
                    near[g * per_grain + b],
                    (((1,), (1,)), ((), ())),
                    preferred_element_type=jnp.float32,
                )
                total = total[:ROWS] + total[ROWS:]
                if step:
                    factor = jnp.exp2(
                        jnp.sum(
                            own_rows[place_ref[g, b]] * own_shift[g], axis=0, keepdims=True
                        )
                    )
                    total = total * factor
                normal_sums[g, b] = total
                rate = jnp.sum(total * velocity[g], axis=0, keepdims=True)
                rates = jnp.where(half == b, rate, rates)
            added[pl.ds(pl.multiple_of(g * per_grain, ROWS), per_grain), :] = rates
            return carry

        lax.fori_loop(0, grains, body, 0)

    def to_fluid(step):
        high, rest = two_parts(added[...])
        spread = jnp.dot(
            one_hot,
            jnp.concatenate([high, rest], axis=1).astype(jnp.bfloat16),
            preferred_element_type=jnp.float32,
        )
        spread = spread[:, :lanes] + spread[:, lanes:]
        give[step] = spread.reshape(tiles, cells, lanes)
        return [
            ship(
                give.at[step, r],
                take.at[step, r],
                take_send.at[step, r],
                take_recv.at[step, r],
                group_back(r),
            )
            for r in reversed(order)
        ]

    def collect(step, copies):
        total = give[step, 0]
        for copy in copies:
            copy.wait_recv()
        for r in range(1, tiles):
            total = total + take[step, r]
        return total

    merged = size_x == 1 and n_flow == 2
    sources = {("own", 0): 0}
    flow_keys = [("flow", 1)] if merged else [("flow", 1), ("flow", -1)]
    for key in flow_keys + [("cross", 1), ("cross", -1), ("depth", 1), ("depth", -1)]:
        sources[key] = len(sources)
    outer_keys = [key for key in sources if key[0] != "own"]

    def columns_of(keys, pick):
        rows = []
        for axis, side in keys:
            if axis == "own":
                rows.append(pick(0, None))
            elif axis == "flow":
                rows.append(pick(slot_flow[side], None))
            elif axis == "cross":
                rows.append(pick(slot_cross[side], None))
            else:
                rows.append(pick(None, depth_index[side]))
        spare = -len(keys) * cells % 128
        if spare:
            rows.append(jnp.zeros((spare, lanes), jnp.float32))
        return jnp.transpose(jnp.concatenate(rows, axis=0))

    def pairs(cell):
        x, rest = divmod(cell, size_y * size_z)
        y, z = divmod(rest, size_z)
        found = [(cell, (0, 0, 0))]
        place, extent, names = (x, y, z), (size_x, size_y, size_z), ("flow", "cross", "depth")
        for axis in range(3):
            for side in (1, -1):
                near = list(place)
                near[axis] += side
                key = ("own", 0)
                if not 0 <= near[axis] < extent[axis]:
                    near[axis] %= extent[axis]
                    key = (names[axis], side)
                    if axis == 0 and merged:
                        key = (names[axis], 1)
                index = (near[0] * size_y + near[1]) * size_z + near[2]
                step = [0, 0, 0]
                step[axis] = side
                found.append((sources[key] * cells + index, tuple(step)))
        return found

    groups = []
    for cell in range(cells):
        by_column = {}
        for column, step in pairs(cell):
            by_column.setdefault(column, []).append(step)
        groups.append(list(by_column.items()))

    start = jnp.zeros((ROWS, grains), jnp.float32)
    grain_row = lax.broadcasted_iota(jnp.int32, (ROWS, grains), 0)
    for c in range(3):
        start = jnp.where(grain_row == c, start_ref[c : c + 1, :], start)
    for g in range(grains):
        speed_rows[g] = jnp.broadcast_to(start[:, g : g + 1], (ROWS, lanes))
        mass_rows[g] = jnp.broadcast_to(mass_ref[:, g : g + 1], (ROWS, lanes))
        moved_rows[g] = jnp.zeros((ROWS, lanes), jnp.float32)

    weigh(0, speed_rows, None, None)
    copies = to_fluid(0)
    for copy in off_depth_copies:
        copy.wait_recv()

    turned = [
        SCALE
        * columns_of(
            list(sources),
            lambda slot, i, c=c: (
                off_group[slot, c * cells : (c + 1) * cells, :]
                if i is None
                else off_depth[i, c * cells : (c + 1) * cells, :]
            )
        )
        for c in range(3)
    ]
    sum_rows = []
    for cell in range(cells):
        own = [
            SCALE * off_ref[c * cells + cell : c * cells + cell + 1, :] for c in range(3)
        ]
        full = None
        for position, (column, steps) in enumerate(groups[cell]):
            total = None
            for step in steps:
                weight = weight_of(
                    [
                        turned[c][:, column : column + 1] - (own[c] - SCALE * step[c])
                        for c in range(3)
                    ]
                )
                total = weight if total is None else total + weight
            weights[cell, position] = total
            full = total if full is None else full + total
        sum_rows.append(jnp.sum(full, axis=0, keepdims=True))
    rowsum = jnp.concatenate(sum_rows, axis=0)
    diagonal = STIFFEN + rowsum - PER_PARTICLE
    inverse = 1.0 / diagonal

    def products(columns, base, inside):
        rows = []
        for cell in range(cells):
            total = None
            for low in range(0, lanes, 64):
                acc = None
                for position, (column, _) in enumerate(groups[cell]):
                    if (column < cells) != inside:
                        continue
                    term = (
                        weights[cell, position, low : low + 64, :]
                        * columns[low : low + 64, column - base : column - base + 1]
                    )
                    acc = term if acc is None else acc + term
                acc = jnp.sum(acc.reshape(8, 8, lanes), axis=0)
                total = acc if total is None else total + acc
            rows.append(jnp.sum(total, axis=0, keepdims=True))
        return jnp.concatenate(rows, axis=0)

    def inner(field):
        return products(columns_of([("own", 0)], lambda slot, i: field), 0, True)

    def outer(step, j):
        columns = columns_of(
            outer_keys,
            lambda slot, i: krylov[step, j, slot] if i is None else krylov_depth[step, j, i],
        )
        return products(columns, cells, False)

    pressure = jnp.zeros((cells, lanes), jnp.float32)
    spread_before = None
    residual = None
    pressure_all = None
    corner = lax.broadcasted_iota(
        jnp.int32, (2 * ITERS, lanes), 0
    ) == lax.broadcasted_iota(jnp.int32, (2 * ITERS, lanes), 1)
    for step in range(STEPS):
        if step:
            for g in range(grains):
                shift = SCALE * moved_rows[g]
                square = 0.5 * jnp.sum(shift * shift, axis=0, keepdims=True)
                own_shift[g] = jnp.where(row == 3, square, shift)
                point_shift[g] = jnp.where(row == 4, -square, -2.0 * shift)
            weigh(step, speed_rows, own_shift, point_shift)
            copies = to_fluid(step)
        spread = collect(step, copies)
        if step == 0:
            residual = source_ref[...] + spread
        else:
            residual = residual + (spread - spread_before)
        spread_before = spread
        fields = [residual * inverse]
        far = []
        for j in range(ITERS):
            krylov[step, j, 0] = fields[j]
            close = {}
            for r in near_slots:
                close[r] = ship(
                    krylov.at[step, j, 0],
                    krylov.at[step, j, r],
                    kry_send.at[step, j, r],
                    kry_recv.at[step, j, r],
                    group_at(r),
                )
            beside = [
                ship(
                    krylov.at[step, j, 0],
                    krylov_depth.at[step, j, i],
                    kry_send.at[step, j, tiles + i],
                    kry_recv.at[step, j, tiles + i],
                    depth_at(rd),
                )
                for i, rd in enumerate(near_depth)
            ]
            for r in far_slots:
                far.append(
                    ship(
                        krylov.at[step, j, 0],
                        krylov.at[step, j, r],
                        kry_send.at[step, j, r],
                        kry_recv.at[step, j, r],
                        group_at(r),
                    )
                )
            inside = inner(fields[j]) - PER_PARTICLE * fields[j]
            for copy in list(close.values()) + beside:
                copy.wait_recv()
            fields.append((inside + outer(step, j)) * inverse)
        moments = []
        for j in range(ITERS):
            scaled = diagonal * fields[j]
            moments.append(jnp.sum(scaled * fields[j], axis=0, keepdims=True))
            moments.append(jnp.sum(scaled * fields[j + 1], axis=0, keepdims=True))
        own = jnp.sum(jnp.concatenate(moments, axis=0), axis=1, keepdims=True)
        own = jnp.sum(jnp.where(corner, own, 0.0), axis=0, keepdims=True)
        part[step, 0] = own
        waits = [
            ship(
                part.at[step, 0],
                part.at[step, r * n_depth + rd],
                part_send.at[step, r * n_depth + rd],
                part_recv.at[step, r * n_depth + rd],
                everyone_at(r, rd),
            )
            for r, rd in everyone
        ]
        for copy in waits:
            copy.wait_recv()
        total = jnp.sum(part[step], axis=0)
        total = jnp.sum(jnp.where(corner, total, 0.0), axis=1, keepdims=True)
        total = jnp.broadcast_to(total, (2 * ITERS, lanes))
        scalars = [total[q : q + 1, :] for q in range(2 * ITERS)]
        gram = [
            [scalars[i + j] - scalars[i + j + 1] for j in range(ITERS)] for i in range(ITERS)
        ]
        factors = solve_small(gram, scalars[:ITERS])
        for j in range(ITERS):
            pressure = pressure + factors[j] * fields[j]
            residual = residual - factors[j] * (diagonal * (fields[j] - fields[j + 1]))
        for copy in far:
            copy.wait_recv()
        for j in range(ITERS):
            term = factors[j] * krylov[step, j].reshape(tiles * cells, lanes)
            pressure_all = term if pressure_all is None else pressure_all + term
        felt_rows[...] = pressure_all

        def push(g, carry):
            total = None
            for b in range(per_grain):
                felt = felt_rows[pl.ds(place_ref[g, b], 1), :]
                term = normal_sums[g, b] * felt
                total = term if total is None else total + term
            force = jnp.broadcast_to(
                jnp.sum(total, axis=1, keepdims=True), (ROWS, lanes)
            )
            speed = speed_rows[g] + STEP_TIME * force / mass_rows[g]
            speed_rows[g] = speed
            moved_rows[g] = moved_rows[g] + STEP_TIME * speed
            return carry

        lax.fori_loop(0, grains, push, 0)
    press_out[...] = pressure
    lane = lax.broadcasted_iota(jnp.int32, (ROWS, lanes), 1)
    speed = jnp.zeros((ROWS, lanes), jnp.float32)
    for g in range(grains):
        speed = jnp.where(lane == g, speed_rows[g], speed)
    speed_out[...] = speed[:3, :grains]
    for copy in sent:
        copy.wait_send()


def per_device(
    sizes,
    fluid_offsets,
    source,
    marker_offsets,
    marker_normals,
    dest_tile,
    cell_index,
    grain_velocity,
    grain_mass,
):
    n_flow, n_cross, n_depth = sizes
    tiles = n_flow * n_cross
    dims = source.shape[:3]
    cells = dims[0] * dims[1] * dims[2]
    lanes = source.shape[3]
    grains, per_grain = cell_index.shape
    blocks = grains * per_grain
    near_count = len({1, n_depth - 1})
    vmem, dma = pltpu.VMEM, pltpu.SemaphoreType.DMA
    f32 = jnp.float32
    in_vmem = pl.BlockSpec(memory_space=pltpu.VMEM)
    pressure, speed = pl.pallas_call(
        functools.partial(kernel, sizes, dims),
        out_shape=(
            jax.ShapeDtypeStruct((cells, lanes), f32),
            jax.ShapeDtypeStruct((3, grains), f32),
        ),
        in_specs=[in_vmem] * 8,
        out_specs=(in_vmem, in_vmem),
        scratch_shapes=[
            vmem((tiles, 3 * cells, lanes), f32),
            vmem((near_count, 3 * cells, lanes), f32),
            vmem((cells, 7, lanes, lanes), f32),
            vmem((tiles * cells, ROWS, lanes), f32),
            vmem((tiles * cells // GROUP, lanes, 4 * ROWS * GROUP), jnp.bfloat16),
            vmem((grains, per_grain, ROWS, lanes), f32),
            vmem((grains, per_grain, 2 * ROWS, lanes), jnp.bfloat16),
            vmem((grains, per_grain, ROWS, lanes), f32),
            vmem((grains, per_grain, 2 * ROWS, lanes), jnp.bfloat16),
            vmem((blocks, lanes, 2 * lanes), jnp.bfloat16),
            vmem((grains, per_grain, ROWS, lanes), f32),
            vmem((blocks, lanes), f32),
            vmem((tiles * cells, lanes), f32),
            vmem((grains, ROWS, lanes), f32),
            vmem((grains, ROWS, lanes), f32),
            vmem((grains, ROWS, lanes), f32),
            vmem((grains, ROWS, lanes), f32),
            vmem((grains, ROWS, lanes), f32),
            vmem((grains, lanes), jnp.int32),
            pltpu.SMEM((grains, lanes), jnp.int32),
            vmem((STEPS, tiles, cells, lanes), f32),
            vmem((STEPS, tiles, cells, lanes), f32),
            vmem((STEPS, ITERS, tiles, cells, lanes), f32),
            vmem((STEPS, ITERS, near_count, cells, lanes), f32),
            vmem((STEPS, tiles * n_depth, 1, lanes), f32),
            dma((tiles + near_count,)),
            dma((tiles + near_count,)),
            dma((STEPS, tiles)),
            dma((STEPS, tiles)),
            dma((STEPS, ITERS, tiles + near_count)),
            dma((STEPS, ITERS, tiles + near_count)),
            dma((STEPS, tiles * n_depth)),
            dma((STEPS, tiles * n_depth)),
            dma,
        ],
        compiler_params=pltpu.CompilerParams(
            collective_id=0, has_side_effects=True, vmem_limit_bytes=60 * 1024 * 1024
        ),
        name="coupled",
    )(
        fluid_offsets.reshape(3 * cells, lanes),
        source.reshape(cells, lanes),
        jnp.transpose(marker_offsets, (0, 2, 1, 3)),
        jnp.transpose(marker_normals, (0, 2, 1, 3)),
        jnp.transpose(dest_tile, (0, 2, 1)),
        cell_index,
        jnp.transpose(grain_velocity),
        grain_mass[None, :],
    )
    return (pressure.reshape(source.shape), jnp.transpose(speed))


def solution(mesh):
    sizes = tuple(mesh.shape[name] for name in ("flow", "cross", "depth"))
    return jax.shard_map(
        functools.partial(per_device, sizes),
        mesh=mesh,
        in_specs=(
            P(None, "flow", "cross", "depth", None),
            P("flow", "cross", "depth", None),
            P(("flow", "cross", "depth"), None, None, None),
            P(("flow", "cross", "depth"), None, None, None),
            P(("flow", "cross", "depth"), None, None),
            P(("flow", "cross", "depth"), None),
            P(("flow", "cross", "depth"), None),
            P(("flow", "cross", "depth")),
        ),
        out_specs=(P("flow", "cross", "depth", None), P(("flow", "cross", "depth"), None)),
        check_vma=False,
    )
```

```python
import functools
import math

import jax
import jax.numpy as jnp
from jax import lax
from jax.experimental import pallas as pl
from jax.experimental.pallas import tpu as pltpu
from jax.sharding import PartitionSpec as P

ITERS = 4
STEPS = 2
STIFFEN = 0.5
STEP_TIME = 0.05
PER_PARTICLE = 1.0 / 128.0
SCALE = math.sqrt(math.log2(math.e))
SHIFT = math.log2(PER_PARTICLE)
MESH = pl.DeviceIdType.MESH
ROWS = 8
GROUP = 4
MIDDLE = 0.5


def weight_of(gaps):
    total = None
    for gap in gaps:
        total = gap * gap if total is None else total + gap * gap
    return jnp.exp2(SHIFT - total)


def rounded(value):
    return value.astype(jnp.bfloat16).astype(jnp.float32)


def solve_small(gram, right):
    n = len(right)
    gram = [list(row) for row in gram]
    right = list(right)
    for i in range(n):
        inverse = 1.0 / gram[i][i]
        for j in range(i + 1, n):
            factor = gram[j][i] * inverse
            for k in range(i + 1, n):
                gram[j][k] = gram[j][k] - factor * gram[i][k]
            right[j] = right[j] - factor * right[i]
    out = [None] * n
    for i in reversed(range(n)):
        value = right[i]
        for k in range(i + 1, n):
            value = value - gram[i][k] * out[k]
        out[i] = value / gram[i][i]
    return out


def two_parts(value):
    high = rounded(value)
    return high, value - high


def kernel(
    sizes,
    dims,
    off_ref,
    source_ref,
    points_ref,
    normals_ref,
    tile_ref,
    cell_ref,
    start_ref,
    mass_ref,
    press_out,
    speed_out,
    off_group,
    off_depth,
    weights,
    own_rows,
    own_parts,
    point_rows,
    point_columns,
    normal_rows,
    normal_parts,
    near,
    normal_sums,
    added,
    felt_rows,
    speed_rows,
    mass_rows,
    moved_rows,
    own_shift,
    point_shift,
    place_rows,
    place_ref,
    give,
    take,
    krylov,
    krylov_depth,
    part,
    off_send,
    off_recv,
    take_send,
    take_recv,
    kry_send,
    kry_recv,
    part_send,
    part_recv,
    place_sem,
):
    n_flow, n_cross, n_depth = sizes
    size_x, size_y, size_z = dims
    cells = size_x * size_y * size_z
    tiles = n_flow * n_cross
    grains, _, per_grain, lanes = points_ref.shape
    blocks = grains * per_grain
    flow, cross, depth = (lax.axis_index("flow"), lax.axis_index("cross"), lax.axis_index("depth"))

    def group_at(slot):
        rf, rc = divmod(slot, n_cross)
        return (lax.rem(flow + rf, n_flow), lax.rem(cross + rc, n_cross), depth)

    def group_back(slot):
        rf, rc = divmod(slot, n_cross)
        return (
            lax.rem(flow + n_flow - rf, n_flow),
            lax.rem(cross + n_cross - rc, n_cross),
            depth,
        )

    def depth_at(rd):
        return (flow, cross, lax.rem(depth + rd, n_depth))

    slot_flow = {1: (n_flow - 1) * n_cross, -1: (1 % n_flow) * n_cross}
    slot_cross = {1: n_cross - 1, -1: 1 % n_cross}
    near_slots = sorted({slot_flow[1], slot_flow[-1], slot_cross[1], slot_cross[-1]} - {0})
    far_slots = [r for r in range(1, tiles) if r not in near_slots]
    near_slots = sorted(near_slots, key=lambda r: r // n_cross)
    order = near_slots + far_slots
    near_depth = sorted({1, n_depth - 1})
    depth_index = {1: near_depth.index(n_depth - 1), -1: near_depth.index(1)}

    barrier = pltpu.get_barrier_semaphore()
    def everyone_at(r, rd):
        there = group_at(r)
        return (there[0], there[1], lax.rem(depth + rd, n_depth))

    everyone = [(r, rd) for r in [0] + order for rd in range(n_depth) if (r, rd) != (0, 0)]
    everyone = everyone[::-1]
    for r, rd in everyone:
        pl.semaphore_signal(barrier, inc=1, device_id=everyone_at(r, rd), device_id_type=MESH)

    row = lax.broadcasted_iota(jnp.int32, (ROWS, lanes), 0)

    tile = tile_ref[:, 0, :]
    slot_flow_of = lax.rem(flow + n_flow - lax.div(tile, n_cross), n_flow)
    slot_cross_of = lax.rem(cross + n_cross - lax.rem(tile, n_cross), n_cross)
    slot_of = slot_flow_of * n_cross + slot_cross_of
    place_rows[...] = jnp.zeros(place_rows.shape, jnp.int32)
    place_rows[:, :per_grain] = slot_of * cells + cell_ref[...]
    place_copy = pltpu.make_async_copy(place_rows, place_ref, place_sem)
    place_copy.start()

    spot = lax.broadcasted_iota(jnp.int32, (per_grain, blocks), 1)
    pick = (
        lax.rem(spot, per_grain) == lax.broadcasted_iota(jnp.int32, (per_grain, blocks), 0)
    ).astype(jnp.bfloat16)
    held = (
        lax.div(lax.broadcasted_iota(jnp.int32, (grains, blocks), 1), per_grain)
        == lax.broadcasted_iota(jnp.int32, (grains, blocks), 0)
    )

    def in_a_row(value):
        spread = jnp.dot(
            value.astype(jnp.float32).astype(jnp.bfloat16),
            pick,
            preferred_element_type=jnp.float32,
        )
        return jnp.sum(jnp.where(held, spread, 0.0), axis=0, keepdims=True)

    place_row = in_a_row(slot_of) * cells + in_a_row(cell_ref[...])
    one_hot = jnp.where(
        lax.broadcasted_iota(jnp.int32, (tiles * cells, blocks), 0).astype(jnp.float32)
        == place_row,
        1.0,
        0.0,
    ).astype(jnp.bfloat16)

    def prepare(g, carry):
        stacked = []
        for b in range(per_grain):
            point = jnp.where(row > 3, 1.0, 0.0)
            normal = jnp.zeros((ROWS, lanes), jnp.float32)
            for c in range(3):
                point = jnp.where(
                    row == c, SCALE * (points_ref[g, c, b : b + 1, :] - MIDDLE), point
                )
                normal = jnp.where(row == c, normals_ref[g, c, b : b + 1, :], normal)
            square = jnp.sum(jnp.where(row < 3, point * point, 0.0), axis=0, keepdims=True)
            point = jnp.where(row == 3, square, point)
            point_rows[g, b] = point
            high, rest = two_parts(point)
            stacked += [high, rest, high, rest]
            if b % GROUP == GROUP - 1:
                point_columns[g * (per_grain // GROUP) + b // GROUP] = jnp.transpose(
                    jnp.concatenate(stacked, axis=0)
                ).astype(jnp.bfloat16)
                stacked = []
            normal_rows[g, b] = normal
            normal_parts[g, b] = jnp.concatenate(two_parts(normal), axis=0).astype(jnp.bfloat16)
        return carry

    lax.fori_loop(0, grains, prepare, 0)
    place_copy.wait()
    pl.semaphore_wait(barrier, len(everyone))

    sent = []

    def ship(src, dst, send_sem, recv_sem, device):
        copy = pltpu.make_async_remote_copy(
            src_ref=src,
            dst_ref=dst,
            send_sem=send_sem,
            recv_sem=recv_sem,
            device_id=device,
            device_id_type=MESH,
        )
        copy.start()
        sent.append(copy)
        return copy

    off_copies = {}
    for r in order:
        off_copies[r] = ship(
            off_ref, off_group.at[r], off_send.at[r], off_recv.at[r], group_at(r)
        )
    off_depth_copies = []
    for i, rd in enumerate(near_depth):
        off_depth_copies.append(
            ship(
                off_ref,
                off_depth.at[i],
                off_send.at[tiles + i],
                off_recv.at[tiles + i],
                depth_at(rd),
            )
        )
    off_group[0] = off_ref[...]

    def own_pass(slot, carry):
        for cell in range(cells):
            base = jnp.where(row == 3, -1.0, jnp.where(row == 5, SHIFT, 0.0))
            square = None
            for c in range(3):
                spot = c * cells + cell
                own = SCALE * (off_group[slot, spot : spot + 1, :] - MIDDLE)
                base = jnp.where(row == c, 2.0 * own, base)
                square = own * own if square is None else square + own * own
            base = jnp.where(row == 4, -square, base)
            own_rows[slot * cells + cell] = base
            high, rest = two_parts(base)
            own_parts[slot * cells + cell] = jnp.concatenate(
                [high, high, rest, rest], axis=0
            ).astype(jnp.bfloat16)
        return carry

    for r in order:
        off_copies[r].wait_recv()
    lax.fori_loop(0, tiles, own_pass, 0)

    def near_pass(g, carry):
        blank = jnp.zeros((4 * ROWS, lanes), jnp.bfloat16)
        for b in range(per_grain):
            stacked = [blank] * GROUP
            stacked[b % GROUP] = own_parts[place_ref[g, b]]
            weight = jnp.exp2(
                jnp.dot(
                    point_columns[g * (per_grain // GROUP) + b // GROUP],
                    jnp.concatenate(stacked, axis=0),
                    preferred_element_type=jnp.float32,
                )
            )
            upper = weight.astype(jnp.bfloat16)
            near[g * per_grain + b, :lanes, :] = upper
            near[g * per_grain + b, lanes:, :] = (weight - upper.astype(jnp.float32)).astype(
                jnp.bfloat16
            )
        return carry

    lax.fori_loop(0, grains, near_pass, 0)

    def weigh(step, velocity, own_shift, point_shift):
        def body(g, carry):
            rows = []
            half = lax.broadcasted_iota(jnp.int32, (per_grain, lanes), 0)
            rates = jnp.zeros((per_grain, lanes), jnp.float32)
            for b in range(per_grain):
                if step:
                    factor = jnp.exp2(
                        jnp.sum(point_rows[g, b] * point_shift[g], axis=0, keepdims=True)
                    )
                    parts = jnp.concatenate(
                        two_parts(normal_rows[g, b] * factor), axis=0
                    ).astype(jnp.bfloat16)
                else:
                    parts = normal_parts[g, b]
                total = jnp.dot(
                    jnp.concatenate([parts, parts], axis=1),
                    near[g * per_grain + b],
                    preferred_element_type=jnp.float32,
                )
                total = total[:ROWS] + total[ROWS:]
                if step:
                    factor = jnp.exp2(
                        jnp.sum(
                            own_rows[place_ref[g, b]] * own_shift[g], axis=0, keepdims=True
                        )
                    )
                    total = total * factor
                normal_sums[g, b] = total
                rate = jnp.sum(total * velocity[g], axis=0, keepdims=True)
                rates = jnp.where(half == b, rate, rates)
            added[pl.ds(pl.multiple_of(g * per_grain, ROWS), per_grain), :] = rates
            return carry

        lax.fori_loop(0, grains, body, 0)

    def to_fluid(step):
        high, rest = two_parts(added[...])
        spread = jnp.dot(
            one_hot,
            jnp.concatenate([high, rest], axis=1).astype(jnp.bfloat16),
            preferred_element_type=jnp.float32,
        )
        spread = spread[:, :lanes] + spread[:, lanes:]
        give[step] = spread.reshape(tiles, cells, lanes)
        return [
            ship(
                give.at[step, r],
                take.at[step, r],
                take_send.at[step, r],
                take_recv.at[step, r],
                group_back(r),
            )
            for r in reversed(order)
        ]

    def collect(step, copies):
        total = give[step, 0]
        for copy in copies:
            copy.wait_recv()
        for r in range(1, tiles):
            total = total + take[step, r]
        return total

    merged = size_x == 1 and n_flow == 2
    sources = {("own", 0): 0}
    flow_keys = [("flow", 1)] if merged else [("flow", 1), ("flow", -1)]
    for key in flow_keys + [("cross", 1), ("cross", -1), ("depth", 1), ("depth", -1)]:
        sources[key] = len(sources)
    outer_keys = [key for key in sources if key[0] != "own"]

    def columns_of(keys, pick):
        rows = []
        for axis, side in keys:
            if axis == "own":
                rows.append(pick(0, None))
            elif axis == "flow":
                rows.append(pick(slot_flow[side], None))
            elif axis == "cross":
                rows.append(pick(slot_cross[side], None))
            else:
                rows.append(pick(None, depth_index[side]))
        spare = -len(keys) * cells % 128
        if spare:
            rows.append(jnp.zeros((spare, lanes), jnp.float32))
        return jnp.transpose(jnp.concatenate(rows, axis=0))

    def pairs(cell):
        x, rest = divmod(cell, size_y * size_z)
        y, z = divmod(rest, size_z)
        found = [(cell, (0, 0, 0))]
        place, extent, names = (x, y, z), (size_x, size_y, size_z), ("flow", "cross", "depth")
        for axis in range(3):
            for side in (1, -1):
                near = list(place)
                near[axis] += side
                key = ("own", 0)
                if not 0 <= near[axis] < extent[axis]:
                    near[axis] %= extent[axis]
                    key = (names[axis], side)
                    if axis == 0 and merged:
                        key = (names[axis], 1)
                index = (near[0] * size_y + near[1]) * size_z + near[2]
                step = [0, 0, 0]
                step[axis] = side
                found.append((sources[key] * cells + index, tuple(step)))
        return found

    groups = []
    for cell in range(cells):
        by_column = {}
        for column, step in pairs(cell):
            by_column.setdefault(column, []).append(step)
        groups.append(list(by_column.items()))

    start = jnp.zeros((ROWS, grains), jnp.float32)
    grain_row = lax.broadcasted_iota(jnp.int32, (ROWS, grains), 0)
    for c in range(3):
        start = jnp.where(grain_row == c, start_ref[c : c + 1, :], start)
    for g in range(grains):
        speed_rows[g] = jnp.broadcast_to(start[:, g : g + 1], (ROWS, lanes))
        mass_rows[g] = jnp.broadcast_to(mass_ref[:, g : g + 1], (ROWS, lanes))
        moved_rows[g] = jnp.zeros((ROWS, lanes), jnp.float32)

    weigh(0, speed_rows, None, None)
    copies = to_fluid(0)
    for copy in off_depth_copies:
        copy.wait_recv()

    turned = [
        SCALE
        * columns_of(
            list(sources),
            lambda slot, i, c=c: (
                off_group[slot, c * cells : (c + 1) * cells, :]
                if i is None
                else off_depth[i, c * cells : (c + 1) * cells, :]
            )
        )
        for c in range(3)
    ]
    sum_rows = []
    for cell in range(cells):
        own = [
            SCALE * off_ref[c * cells + cell : c * cells + cell + 1, :] for c in range(3)
        ]
        full = None
        for position, (column, steps) in enumerate(groups[cell]):
            total = None
            for step in steps:
                weight = weight_of(
                    [
                        turned[c][:, column : column + 1] - (own[c] - SCALE * step[c])
                        for c in range(3)
                    ]
                )
                total = weight if total is None else total + weight
            weights[cell, position] = total
            full = total if full is None else full + total
        sum_rows.append(jnp.sum(full, axis=0, keepdims=True))
    rowsum = jnp.concatenate(sum_rows, axis=0)
    diagonal = STIFFEN + rowsum - PER_PARTICLE
    inverse = 1.0 / diagonal

    def products(columns, base, inside):
        rows = []
        for cell in range(cells):
            total = None
            for low in range(0, lanes, 64):
                acc = None
                for position, (column, _) in enumerate(groups[cell]):
                    if (column < cells) != inside:
                        continue
                    term = (
                        weights[cell, position, low : low + 64, :]
                        * columns[low : low + 64, column - base : column - base + 1]
                    )
                    acc = term if acc is None else acc + term
                acc = jnp.sum(acc.reshape(8, 8, lanes), axis=0)
                total = acc if total is None else total + acc
            rows.append(jnp.sum(total, axis=0, keepdims=True))
        return jnp.concatenate(rows, axis=0)

    def inner(field):
        return products(columns_of([("own", 0)], lambda slot, i: field), 0, True)

    def outer(step, j):
        columns = columns_of(
            outer_keys,
            lambda slot, i: krylov[step, j, slot] if i is None else krylov_depth[step, j, i],
        )
        return products(columns, cells, False)

    pressure = jnp.zeros((cells, lanes), jnp.float32)
    spread_before = None
    residual = None
    pressure_all = None
    corner = lax.broadcasted_iota(
        jnp.int32, (2 * ITERS, lanes), 0
    ) == lax.broadcasted_iota(jnp.int32, (2 * ITERS, lanes), 1)
    for step in range(STEPS):
        if step:
            for g in range(grains):
                shift = SCALE * moved_rows[g]
                square = 0.5 * jnp.sum(shift * shift, axis=0, keepdims=True)
                own_shift[g] = jnp.where(row == 3, square, shift)
                point_shift[g] = jnp.where(row == 4, -square, -2.0 * shift)
            weigh(step, speed_rows, own_shift, point_shift)
            copies = to_fluid(step)
        spread = collect(step, copies)
        if step == 0:
            residual = source_ref[...] + spread
        else:
            residual = residual + (spread - spread_before)
        spread_before = spread
        fields = [residual * inverse]
        far = []
        for j in range(ITERS):
            krylov[step, j, 0] = fields[j]
            close = {}
            for r in near_slots:
                close[r] = ship(
                    krylov.at[step, j, 0],
                    krylov.at[step, j, r],
                    kry_send.at[step, j, r],
                    kry_recv.at[step, j, r],
                    group_at(r),
                )
            beside = [
                ship(
                    krylov.at[step, j, 0],
                    krylov_depth.at[step, j, i],
                    kry_send.at[step, j, tiles + i],
                    kry_recv.at[step, j, tiles + i],
                    depth_at(rd),
                )
                for i, rd in enumerate(near_depth)
            ]
            for r in far_slots:
                far.append(
                    ship(
                        krylov.at[step, j, 0],
                        krylov.at[step, j, r],
                        kry_send.at[step, j, r],
                        kry_recv.at[step, j, r],
                        group_at(r),
                    )
                )
            inside = inner(fields[j]) - PER_PARTICLE * fields[j]
            for copy in list(close.values()) + beside:
                copy.wait_recv()
            fields.append((inside + outer(step, j)) * inverse)
        moments = []
        for j in range(ITERS):
            scaled = diagonal * fields[j]
            moments.append(jnp.sum(scaled * fields[j], axis=0, keepdims=True))
            moments.append(jnp.sum(scaled * fields[j + 1], axis=0, keepdims=True))
        own = jnp.sum(jnp.concatenate(moments, axis=0), axis=1, keepdims=True)
        own = jnp.sum(jnp.where(corner, own, 0.0), axis=0, keepdims=True)
        part[step, 0] = own
        waits = [
            ship(
                part.at[step, 0],
                part.at[step, r * n_depth + rd],
                part_send.at[step, r * n_depth + rd],
                part_recv.at[step, r * n_depth + rd],
                everyone_at(r, rd),
            )
            for r, rd in everyone
        ]
        for copy in waits:
            copy.wait_recv()
        total = jnp.sum(part[step], axis=0)
        total = jnp.sum(jnp.where(corner, total, 0.0), axis=1, keepdims=True)
        total = jnp.broadcast_to(total, (2 * ITERS, lanes))
        scalars = [total[q : q + 1, :] for q in range(2 * ITERS)]
        gram = [
            [scalars[i + j] - scalars[i + j + 1] for j in range(ITERS)] for i in range(ITERS)
        ]
        factors = solve_small(gram, scalars[:ITERS])
        for j in range(ITERS):
            pressure = pressure + factors[j] * fields[j]
            residual = residual - factors[j] * (diagonal * (fields[j] - fields[j + 1]))
        for copy in far:
            copy.wait_recv()
        for j in range(ITERS):
            term = factors[j] * krylov[step, j].reshape(tiles * cells, lanes)
            pressure_all = term if pressure_all is None else pressure_all + term
        felt_rows[...] = pressure_all

        def push(g, carry):
            total = None
            for b in range(per_grain):
                felt = felt_rows[pl.ds(place_ref[g, b], 1), :]
                term = normal_sums[g, b] * felt
                total = term if total is None else total + term
            force = jnp.broadcast_to(
                jnp.sum(total, axis=1, keepdims=True), (ROWS, lanes)
            )
            speed = speed_rows[g] + STEP_TIME * force / mass_rows[g]
            speed_rows[g] = speed
            moved_rows[g] = moved_rows[g] + STEP_TIME * speed
            return carry

        lax.fori_loop(0, grains, push, 0)
    press_out[...] = pressure
    lane = lax.broadcasted_iota(jnp.int32, (ROWS, lanes), 1)
    speed = jnp.zeros((ROWS, lanes), jnp.float32)
    for g in range(grains):
        speed = jnp.where(lane == g, speed_rows[g], speed)
    speed_out[...] = speed[:3, :grains]
    for copy in sent:
        copy.wait_send()


def per_device(
    sizes,
    fluid_offsets,
    source,
    marker_offsets,
    marker_normals,
    dest_tile,
    cell_index,
    grain_velocity,
    grain_mass,
):
    n_flow, n_cross, n_depth = sizes
    tiles = n_flow * n_cross
    dims = source.shape[:3]
    cells = dims[0] * dims[1] * dims[2]
    lanes = source.shape[3]
    grains, per_grain = cell_index.shape
    blocks = grains * per_grain
    near_count = len({1, n_depth - 1})
    vmem, dma = pltpu.VMEM, pltpu.SemaphoreType.DMA
    f32 = jnp.float32
    in_vmem = pl.BlockSpec(memory_space=pltpu.VMEM)
    pressure, speed = pl.pallas_call(
        functools.partial(kernel, sizes, dims),
        out_shape=(
            jax.ShapeDtypeStruct((cells, lanes), f32),
            jax.ShapeDtypeStruct((3, grains), f32),
        ),
        in_specs=[in_vmem] * 8,
        out_specs=(in_vmem, in_vmem),
        scratch_shapes=[
            vmem((tiles, 3 * cells, lanes), f32),
            vmem((near_count, 3 * cells, lanes), f32),
            vmem((cells, 7, lanes, lanes), f32),
            vmem((tiles * cells, ROWS, lanes), f32),
            vmem((tiles * cells, 4 * ROWS, lanes), jnp.bfloat16),
            vmem((grains, per_grain, ROWS, lanes), f32),
            vmem((blocks // GROUP, lanes, 4 * ROWS * GROUP), jnp.bfloat16),
            vmem((grains, per_grain, ROWS, lanes), f32),
            vmem((grains, per_grain, 2 * ROWS, lanes), jnp.bfloat16),
            vmem((blocks, 2 * lanes, lanes), jnp.bfloat16),
            vmem((grains, per_grain, ROWS, lanes), f32),
            vmem((blocks, lanes), f32),
            vmem((tiles * cells, lanes), f32),
            vmem((grains, ROWS, lanes), f32),
            vmem((grains, ROWS, lanes), f32),
            vmem((grains, ROWS, lanes), f32),
            vmem((grains, ROWS, lanes), f32),
            vmem((grains, ROWS, lanes), f32),
            vmem((grains, lanes), jnp.int32),
            pltpu.SMEM((grains, lanes), jnp.int32),
            vmem((STEPS, tiles, cells, lanes), f32),
            vmem((STEPS, tiles, cells, lanes), f32),
            vmem((STEPS, ITERS, tiles, cells, lanes), f32),
            vmem((STEPS, ITERS, near_count, cells, lanes), f32),
            vmem((STEPS, tiles * n_depth, 1, lanes), f32),
            dma((tiles + near_count,)),
            dma((tiles + near_count,)),
            dma((STEPS, tiles)),
            dma((STEPS, tiles)),
            dma((STEPS, ITERS, tiles + near_count)),
            dma((STEPS, ITERS, tiles + near_count)),
            dma((STEPS, tiles * n_depth)),
            dma((STEPS, tiles * n_depth)),
            dma,
        ],
        compiler_params=pltpu.CompilerParams(
            collective_id=0, has_side_effects=True, vmem_limit_bytes=60 * 1024 * 1024
        ),
        name="coupled",
    )(
        fluid_offsets.reshape(3 * cells, lanes),
        source.reshape(cells, lanes),
        jnp.transpose(marker_offsets, (0, 2, 1, 3)),
        jnp.transpose(marker_normals, (0, 2, 1, 3)),
        jnp.transpose(dest_tile, (0, 2, 1)),
        cell_index,
        jnp.transpose(grain_velocity),
        grain_mass[None, :],
    )
    return (pressure.reshape(source.shape), jnp.transpose(speed))


def solution(mesh):
    sizes = tuple(mesh.shape[name] for name in ("flow", "cross", "depth"))
    return jax.shard_map(
        functools.partial(per_device, sizes),
        mesh=mesh,
        in_specs=(
            P(None, "flow", "cross", "depth", None),
            P("flow", "cross", "depth", None),
            P(("flow", "cross", "depth"), None, None, None),
            P(("flow", "cross", "depth"), None, None, None),
            P(("flow", "cross", "depth"), None, None),
            P(("flow", "cross", "depth"), None),
            P(("flow", "cross", "depth"), None),
            P(("flow", "cross", "depth")),
        ),
        out_specs=(P("flow", "cross", "depth", None), P(("flow", "cross", "depth"), None)),
        check_vma=False,
    )
```

```python
import functools
import math

import jax
import jax.numpy as jnp
from jax import lax
from jax.experimental import pallas as pl
from jax.experimental.pallas import tpu as pltpu
from jax.sharding import PartitionSpec as P

ITERS = 4
STEPS = 2
STIFFEN = 0.5
STEP_TIME = 0.05
PER_PARTICLE = 1.0 / 128.0
SCALE = math.sqrt(math.log2(math.e))
SHIFT = math.log2(PER_PARTICLE)
MESH = pl.DeviceIdType.MESH
ROWS = 8
GROUP = 4
FOLDED = 4
MIDDLE = 0.5


def weight_of(gaps):
    total = None
    for gap in gaps:
        total = gap * gap if total is None else total + gap * gap
    return jnp.exp2(SHIFT - total)


def rounded(value):
    return value.astype(jnp.bfloat16).astype(jnp.float32)


def solve_small(gram, right):
    n = len(right)
    gram = [list(row) for row in gram]
    right = list(right)
    for i in range(n):
        inverse = 1.0 / gram[i][i]
        for j in range(i + 1, n):
            factor = gram[j][i] * inverse
            for k in range(i + 1, n):
                gram[j][k] = gram[j][k] - factor * gram[i][k]
            right[j] = right[j] - factor * right[i]
    out = [None] * n
    for i in reversed(range(n)):
        value = right[i]
        for k in range(i + 1, n):
            value = value - gram[i][k] * out[k]
        out[i] = value / gram[i][i]
    return out


def two_parts(value):
    high = rounded(value)
    return high, value - high


def kernel(
    sizes,
    dims,
    off_ref,
    source_ref,
    points_ref,
    normals_ref,
    tile_ref,
    cell_ref,
    start_ref,
    mass_ref,
    press_out,
    speed_out,
    off_group,
    off_depth,
    weights,
    own_rows,
    own_parts,
    point_rows,
    point_columns,
    normal_rows,
    normal_parts,
    near,
    normal_sums,
    added,
    felt_rows,
    speed_rows,
    mass_rows,
    moved_rows,
    own_shift,
    point_shift,
    place_rows,
    place_ref,
    give,
    take,
    krylov,
    krylov_depth,
    part,
    off_send,
    off_recv,
    take_send,
    take_recv,
    kry_send,
    kry_recv,
    part_send,
    part_recv,
    place_sem,
    press_away,
    press_home,
    press_send,
    press_recv,
):
    n_flow, n_cross, n_depth = sizes
    size_x, size_y, size_z = dims
    cells = size_x * size_y * size_z
    tiles = n_flow * n_cross
    grains, _, per_grain, lanes = points_ref.shape
    blocks = grains * per_grain
    flow, cross, depth = (lax.axis_index("flow"), lax.axis_index("cross"), lax.axis_index("depth"))

    fold = n_cross == FOLDED

    def folded(place):
        if not fold:
            return place
        return place + lax.div(place, 2) * (2 * n_cross - 3 - 2 * place)

    line = folded(cross)

    def home_at(slot):
        rf, rc = divmod(slot, n_cross)
        return (lax.rem(flow + rf, n_flow), lax.rem(cross + rc, n_cross), depth)

    def group_at(slot):
        rf, rc = divmod(slot, n_cross)
        return (lax.rem(flow + rf, n_flow), folded(lax.rem(line + rc, n_cross)), depth)

    def group_back(slot):
        rf, rc = divmod(slot, n_cross)
        return (
            lax.rem(flow + n_flow - rf, n_flow),
            folded(lax.rem(line + n_cross - rc, n_cross)),
            depth,
        )

    def tile_at(slot):
        there = lax.rem(flow + n_flow - lax.div(slot, n_cross), n_flow)
        return there * n_cross + lax.rem(line + n_cross - lax.rem(slot, n_cross), n_cross)

    def depth_at(rd):
        return (flow, cross, lax.rem(depth + rd, n_depth))

    slot_flow = {1: (n_flow - 1) * n_cross, -1: (1 % n_flow) * n_cross}
    slot_cross = {1: n_cross - 1, -1: 1 % n_cross}
    near_slots = sorted({slot_flow[1], slot_flow[-1], slot_cross[1], slot_cross[-1]} - {0})
    far_slots = [r for r in range(1, tiles) if r not in near_slots]
    near_slots = sorted(near_slots, key=lambda r: r // n_cross)
    order = near_slots + far_slots
    near_depth = sorted({1, n_depth - 1})
    depth_index = {1: near_depth.index(n_depth - 1), -1: near_depth.index(1)}

    barrier = pltpu.get_barrier_semaphore()
    def everyone_at(r, rd):
        there = group_at(r)
        return (there[0], there[1], lax.rem(depth + rd, n_depth))

    everyone = [(r, rd) for r in [0] + order for rd in range(n_depth) if (r, rd) != (0, 0)]
    everyone = everyone[::-1]
    for r, rd in everyone:
        pl.semaphore_signal(barrier, inc=1, device_id=everyone_at(r, rd), device_id_type=MESH)

    row = lax.broadcasted_iota(jnp.int32, (ROWS, lanes), 0)

    tile = tile_ref[:, 0, :]
    slot_flow_of = lax.rem(flow + n_flow - lax.div(tile, n_cross), n_flow)
    slot_cross_of = lax.rem(line + n_cross - lax.rem(tile, n_cross), n_cross)
    slot_of = slot_flow_of * n_cross + slot_cross_of
    place_rows[...] = jnp.zeros(place_rows.shape, jnp.int32)
    place_rows[:, :per_grain] = slot_of * cells + cell_ref[...]
    place_copy = pltpu.make_async_copy(place_rows, place_ref, place_sem)
    place_copy.start()

    spot = lax.broadcasted_iota(jnp.int32, (per_grain, blocks), 1)
    pick = (
        lax.rem(spot, per_grain) == lax.broadcasted_iota(jnp.int32, (per_grain, blocks), 0)
    ).astype(jnp.bfloat16)
    held = (
        lax.div(lax.broadcasted_iota(jnp.int32, (grains, blocks), 1), per_grain)
        == lax.broadcasted_iota(jnp.int32, (grains, blocks), 0)
    )

    def in_a_row(value):
        spread = jnp.dot(
            value.astype(jnp.float32).astype(jnp.bfloat16),
            pick,
            preferred_element_type=jnp.float32,
        )
        return jnp.sum(jnp.where(held, spread, 0.0), axis=0, keepdims=True)

    place_row = in_a_row(slot_of) * cells + in_a_row(cell_ref[...])
    one_hot = jnp.where(
        lax.broadcasted_iota(jnp.int32, (tiles * cells, blocks), 0).astype(jnp.float32)
        == place_row,
        1.0,
        0.0,
    ).astype(jnp.bfloat16)

    def prepare(g, carry):
        stacked = []
        for b in range(per_grain):
            point = jnp.where(row > 3, 1.0, 0.0)
            normal = jnp.zeros((ROWS, lanes), jnp.float32)
            for c in range(3):
                point = jnp.where(
                    row == c, SCALE * (points_ref[g, c, b : b + 1, :] - MIDDLE), point
                )
                normal = jnp.where(row == c, normals_ref[g, c, b : b + 1, :], normal)
            square = jnp.sum(jnp.where(row < 3, point * point, 0.0), axis=0, keepdims=True)
            point = jnp.where(row == 3, square, point)
            point_rows[g, b] = point
            high, rest = two_parts(point)
            stacked += [high, rest, high, rest]
            if b % GROUP == GROUP - 1:
                point_columns[g * (per_grain // GROUP) + b // GROUP] = jnp.transpose(
                    jnp.concatenate(stacked, axis=0)
                ).astype(jnp.bfloat16)
                stacked = []
            normal_rows[g, b] = normal
            normal_parts[g, b] = jnp.concatenate(two_parts(normal), axis=0).astype(jnp.bfloat16)
        return carry

    lax.fori_loop(0, grains, prepare, 0)
    place_copy.wait()
    pl.semaphore_wait(barrier, len(everyone))

    sent = []

    def ship(src, dst, send_sem, recv_sem, device):
        copy = pltpu.make_async_remote_copy(
            src_ref=src,
            dst_ref=dst,
            send_sem=send_sem,
            recv_sem=recv_sem,
            device_id=device,
            device_id_type=MESH,
        )
        copy.start()
        sent.append(copy)
        return copy

    home = flow * n_cross + cross
    off_copies = {}
    for r in order:
        off_copies[r] = ship(
            off_ref, off_group.at[home], off_send.at[r], off_recv.at[r], home_at(r)
        )
    off_depth_copies = []
    for i, rd in enumerate(near_depth):
        off_depth_copies.append(
            ship(
                off_ref,
                off_depth.at[i],
                off_send.at[tiles + i],
                off_recv.at[tiles + i],
                (flow, line, lax.rem(depth + rd, n_depth)),
            )
        )
    off_group[home] = off_ref[...]

    def own_pass(slot, carry):
        tile_of = tile_at(slot)
        for cell in range(cells):
            base = jnp.where(row == 3, -1.0, jnp.where(row == 5, SHIFT, 0.0))
            square = None
            for c in range(3):
                spot = c * cells + cell
                own = SCALE * (off_group[tile_of, spot : spot + 1, :] - MIDDLE)
                base = jnp.where(row == c, 2.0 * own, base)
                square = own * own if square is None else square + own * own
            base = jnp.where(row == 4, -square, base)
            own_rows[slot * cells + cell] = base
            high, rest = two_parts(base)
            own_parts[slot * cells + cell] = jnp.concatenate(
                [high, high, rest, rest], axis=0
            ).astype(jnp.bfloat16)
        return carry

    for r in order:
        off_copies[r].wait_recv()
    lax.fori_loop(0, tiles, own_pass, 0)

    def near_pass(g, carry):
        blank = jnp.zeros((4 * ROWS, lanes), jnp.bfloat16)
        for b in range(per_grain):
            stacked = [blank] * GROUP
            stacked[b % GROUP] = own_parts[place_ref[g, b]]
            weight = jnp.exp2(
                jnp.dot(
                    point_columns[g * (per_grain // GROUP) + b // GROUP],
                    jnp.concatenate(stacked, axis=0),
                    preferred_element_type=jnp.float32,
                )
            )
            upper = weight.astype(jnp.bfloat16)
            near[g * per_grain + b, :lanes, :] = upper
            near[g * per_grain + b, lanes:, :] = (weight - upper.astype(jnp.float32)).astype(
                jnp.bfloat16
            )
        return carry

    lax.fori_loop(0, grains, near_pass, 0)

    def weigh(step, velocity, own_shift, point_shift):
        def body(g, carry):
            rows = []
            half = lax.broadcasted_iota(jnp.int32, (per_grain, lanes), 0)
            rates = jnp.zeros((per_grain, lanes), jnp.float32)
            for b in range(per_grain):
                if step:
                    factor = jnp.exp2(
                        jnp.sum(point_rows[g, b] * point_shift[g], axis=0, keepdims=True)
                    )
                    parts = jnp.concatenate(
                        two_parts(normal_rows[g, b] * factor), axis=0
                    ).astype(jnp.bfloat16)
                else:
                    parts = normal_parts[g, b]
                total = jnp.dot(
                    jnp.concatenate([parts, parts], axis=1),
                    near[g * per_grain + b],
                    preferred_element_type=jnp.float32,
                )
                total = total[:ROWS] + total[ROWS:]
                if step:
                    factor = jnp.exp2(
                        jnp.sum(
                            own_rows[place_ref[g, b]] * own_shift[g], axis=0, keepdims=True
                        )
                    )
                    total = total * factor
                normal_sums[g, b] = total
                rate = jnp.sum(total * velocity[g], axis=0, keepdims=True)
                rates = jnp.where(half == b, rate, rates)
            added[pl.ds(pl.multiple_of(g * per_grain, ROWS), per_grain), :] = rates
            return carry

        lax.fori_loop(0, grains, body, 0)

    def to_fluid(step):
        high, rest = two_parts(added[...])
        spread = jnp.dot(
            one_hot,
            jnp.concatenate([high, rest], axis=1).astype(jnp.bfloat16),
            preferred_element_type=jnp.float32,
        )
        spread = spread[:, :lanes] + spread[:, lanes:]
        give[step] = spread.reshape(tiles, cells, lanes)
        own_slot = lax.rem(line + n_cross - cross, n_cross)
        give[step, own_slot] = give[step, own_slot] + source_ref[...]
        return [
            ship(
                give.at[step, r],
                take.at[step, r],
                take_send.at[step, r],
                take_recv.at[step, r],
                group_back(r),
            )
            for r in reversed(order)
        ]

    def collect(step, copies):
        total = give[step, 0]
        for copy in copies:
            copy.wait_recv()
        for r in range(1, tiles):
            total = total + take[step, r]
        return total

    merged = size_x == 1 and n_flow == 2
    sources = {("own", 0): 0}
    flow_keys = [("flow", 1)] if merged else [("flow", 1), ("flow", -1)]
    for key in flow_keys + [("cross", 1), ("cross", -1), ("depth", 1), ("depth", -1)]:
        sources[key] = len(sources)
    outer_keys = [key for key in sources if key[0] != "own"]

    def columns_of(keys, pick):
        rows = []
        for axis, side in keys:
            if axis == "own":
                rows.append(pick(0, None))
            elif axis == "flow":
                rows.append(pick(slot_flow[side], None))
            elif axis == "cross":
                rows.append(pick(slot_cross[side], None))
            else:
                rows.append(pick(None, depth_index[side]))
        spare = -len(keys) * cells % 128
        if spare:
            rows.append(jnp.zeros((spare, lanes), jnp.float32))
        return jnp.transpose(jnp.concatenate(rows, axis=0))

    def pairs(cell):
        x, rest = divmod(cell, size_y * size_z)
        y, z = divmod(rest, size_z)
        found = [(cell, (0, 0, 0))]
        place, extent, names = (x, y, z), (size_x, size_y, size_z), ("flow", "cross", "depth")
        for axis in range(3):
            for side in (1, -1):
                near = list(place)
                near[axis] += side
                key = ("own", 0)
                if not 0 <= near[axis] < extent[axis]:
                    near[axis] %= extent[axis]
                    key = (names[axis], side)
                    if axis == 0 and merged:
                        key = (names[axis], 1)
                index = (near[0] * size_y + near[1]) * size_z + near[2]
                step = [0, 0, 0]
                step[axis] = side
                found.append((sources[key] * cells + index, tuple(step)))
        return found

    groups = []
    for cell in range(cells):
        by_column = {}
        for column, step in pairs(cell):
            by_column.setdefault(column, []).append(step)
        groups.append(list(by_column.items()))

    start = jnp.zeros((ROWS, grains), jnp.float32)
    grain_row = lax.broadcasted_iota(jnp.int32, (ROWS, grains), 0)
    for c in range(3):
        start = jnp.where(grain_row == c, start_ref[c : c + 1, :], start)
    for g in range(grains):
        speed_rows[g] = jnp.broadcast_to(start[:, g : g + 1], (ROWS, lanes))
        mass_rows[g] = jnp.broadcast_to(mass_ref[:, g : g + 1], (ROWS, lanes))
        moved_rows[g] = jnp.zeros((ROWS, lanes), jnp.float32)

    weigh(0, speed_rows, None, None)
    copies = to_fluid(0)
    for copy in off_depth_copies:
        copy.wait_recv()

    turned = [
        SCALE
        * columns_of(
            list(sources),
            lambda slot, i, c=c: (
                off_group[tile_at(slot), c * cells : (c + 1) * cells, :]
                if i is None
                else off_depth[i, c * cells : (c + 1) * cells, :]
            )
        )
        for c in range(3)
    ]
    mine = tile_at(0)
    sum_rows = []
    for cell in range(cells):
        own = [
            SCALE * off_group[mine, c * cells + cell : c * cells + cell + 1, :] for c in range(3)
        ]
        full = None
        for position, (column, steps) in enumerate(groups[cell]):
            total = None
            for step in steps:
                weight = weight_of(
                    [
                        turned[c][:, column : column + 1] - (own[c] - SCALE * step[c])
                        for c in range(3)
                    ]
                )
                total = weight if total is None else total + weight
            weights[cell, position] = total
            full = total if full is None else full + total
        sum_rows.append(jnp.sum(full, axis=0, keepdims=True))
    rowsum = jnp.concatenate(sum_rows, axis=0)
    diagonal = STIFFEN + rowsum - PER_PARTICLE
    inverse = 1.0 / diagonal

    def products(columns, base, inside):
        rows = []
        for cell in range(cells):
            total = None
            for low in range(0, lanes, 64):
                acc = None
                for position, (column, _) in enumerate(groups[cell]):
                    if (column < cells) != inside:
                        continue
                    term = (
                        weights[cell, position, low : low + 64, :]
                        * columns[low : low + 64, column - base : column - base + 1]
                    )
                    acc = term if acc is None else acc + term
                acc = jnp.sum(acc.reshape(8, 8, lanes), axis=0)
                total = acc if total is None else total + acc
            rows.append(jnp.sum(total, axis=0, keepdims=True))
        return jnp.concatenate(rows, axis=0)

    def inner(field):
        return products(columns_of([("own", 0)], lambda slot, i: field), 0, True)

    def outer(step, j):
        columns = columns_of(
            outer_keys,
            lambda slot, i: krylov[step, j, slot] if i is None else krylov_depth[step, j, i],
        )
        return products(columns, cells, False)

    def return_copy():
        return pltpu.make_async_remote_copy(
            src_ref=press_away,
            dst_ref=press_home,
            send_sem=press_send,
            recv_sem=press_recv,
            device_id=(flow, line, depth),
            device_id_type=MESH,
        )

    pressure = jnp.zeros((cells, lanes), jnp.float32)
    spread_before = None
    residual = None
    pressure_all = None
    corner = lax.broadcasted_iota(
        jnp.int32, (2 * ITERS, lanes), 0
    ) == lax.broadcasted_iota(jnp.int32, (2 * ITERS, lanes), 1)
    for step in range(STEPS):
        if step:
            for g in range(grains):
                shift = SCALE * moved_rows[g]
                square = 0.5 * jnp.sum(shift * shift, axis=0, keepdims=True)
                own_shift[g] = jnp.where(row == 3, square, shift)
                point_shift[g] = jnp.where(row == 4, -square, -2.0 * shift)
            weigh(step, speed_rows, own_shift, point_shift)
            copies = to_fluid(step)
        spread = collect(step, copies)
        if step == 0:
            residual = spread
        else:
            residual = residual + (spread - spread_before)
        spread_before = spread
        fields = [residual * inverse]
        far = []
        for j in range(ITERS):
            krylov[step, j, 0] = fields[j]
            close = {}
            for r in near_slots:
                close[r] = ship(
                    krylov.at[step, j, 0],
                    krylov.at[step, j, r],
                    kry_send.at[step, j, r],
                    kry_recv.at[step, j, r],
                    group_at(r),
                )
            beside = [
                ship(
                    krylov.at[step, j, 0],
                    krylov_depth.at[step, j, i],
                    kry_send.at[step, j, tiles + i],
                    kry_recv.at[step, j, tiles + i],
                    depth_at(rd),
                )
                for i, rd in enumerate(near_depth)
            ]
            for r in far_slots:
                far.append(
                    ship(
                        krylov.at[step, j, 0],
                        krylov.at[step, j, r],
                        kry_send.at[step, j, r],
                        kry_recv.at[step, j, r],
                        group_at(r),
                    )
                )
            inside = inner(fields[j]) - PER_PARTICLE * fields[j]
            for copy in list(close.values()) + beside:
                copy.wait_recv()
            fields.append((inside + outer(step, j)) * inverse)
        moments = []
        for j in range(ITERS):
            scaled = diagonal * fields[j]
            moments.append(jnp.sum(scaled * fields[j], axis=0, keepdims=True))
            moments.append(jnp.sum(scaled * fields[j + 1], axis=0, keepdims=True))
        own = jnp.sum(jnp.concatenate(moments, axis=0), axis=1, keepdims=True)
        own = jnp.sum(jnp.where(corner, own, 0.0), axis=0, keepdims=True)
        part[step, 0] = own
        waits = [
            ship(
                part.at[step, 0],
                part.at[step, r * n_depth + rd],
                part_send.at[step, r * n_depth + rd],
                part_recv.at[step, r * n_depth + rd],
                everyone_at(r, rd),
            )
            for r, rd in everyone
        ]
        for copy in waits:
            copy.wait_recv()
        total = jnp.sum(part[step], axis=0)
        total = jnp.sum(jnp.where(corner, total, 0.0), axis=1, keepdims=True)
        total = jnp.broadcast_to(total, (2 * ITERS, lanes))
        scalars = [total[q : q + 1, :] for q in range(2 * ITERS)]
        gram = [
            [scalars[i + j] - scalars[i + j + 1] for j in range(ITERS)] for i in range(ITERS)
        ]
        factors = solve_small(gram, scalars[:ITERS])
        for j in range(ITERS):
            pressure = pressure + factors[j] * fields[j]
            residual = residual - factors[j] * (diagonal * (fields[j] - fields[j + 1]))
        for copy in far:
            copy.wait_recv()
        for j in range(ITERS):
            term = factors[j] * krylov[step, j].reshape(tiles * cells, lanes)
            pressure_all = term if pressure_all is None else pressure_all + term
        if step == STEPS - 1:
            press_out[...] = pressure
        if fold and step == STEPS - 1:
            press_away[...] = pressure

            @pl.when(line != cross)
            def _():
                return_copy().start()

        felt_rows[...] = pressure_all

        def push(g, carry):
            total = None
            for b in range(per_grain):
                felt = felt_rows[pl.ds(place_ref[g, b], 1), :]
                term = normal_sums[g, b] * felt
                total = term if total is None else total + term
            force = jnp.broadcast_to(
                jnp.sum(total, axis=1, keepdims=True), (ROWS, lanes)
            )
            speed = speed_rows[g] + STEP_TIME * force / mass_rows[g]
            speed_rows[g] = speed
            moved_rows[g] = moved_rows[g] + STEP_TIME * speed
            return carry

        lax.fori_loop(0, grains, push, 0)
    if fold:

        @pl.when(line != cross)
        def _():
            return_copy().wait()
            press_out[...] = press_home[...]

    lane = lax.broadcasted_iota(jnp.int32, (ROWS, lanes), 1)
    speed = jnp.zeros((ROWS, lanes), jnp.float32)
    for g in range(grains):
        speed = jnp.where(lane == g, speed_rows[g], speed)
    speed_out[...] = speed[:3, :grains]
    for copy in sent:
        copy.wait_send()


def per_device(
    sizes,
    fluid_offsets,
    source,
    marker_offsets,
    marker_normals,
    dest_tile,
    cell_index,
    grain_velocity,
    grain_mass,
):
    n_flow, n_cross, n_depth = sizes
    tiles = n_flow * n_cross
    dims = source.shape[:3]
    cells = dims[0] * dims[1] * dims[2]
    lanes = source.shape[3]
    grains, per_grain = cell_index.shape
    blocks = grains * per_grain
    near_count = len({1, n_depth - 1})
    vmem, dma = pltpu.VMEM, pltpu.SemaphoreType.DMA
    f32 = jnp.float32
    in_vmem = pl.BlockSpec(memory_space=pltpu.VMEM)
    pressure, speed = pl.pallas_call(
        functools.partial(kernel, sizes, dims),
        out_shape=(
            jax.ShapeDtypeStruct((cells, lanes), f32),
            jax.ShapeDtypeStruct((3, grains), f32),
        ),
        in_specs=[in_vmem] * 8,
        out_specs=(in_vmem, in_vmem),
        scratch_shapes=[
            vmem((tiles, 3 * cells, lanes), f32),
            vmem((near_count, 3 * cells, lanes), f32),
            vmem((cells, 7, lanes, lanes), f32),
            vmem((tiles * cells, ROWS, lanes), f32),
            vmem((tiles * cells, 4 * ROWS, lanes), jnp.bfloat16),
            vmem((grains, per_grain, ROWS, lanes), f32),
            vmem((blocks // GROUP, lanes, 4 * ROWS * GROUP), jnp.bfloat16),
            vmem((grains, per_grain, ROWS, lanes), f32),
            vmem((grains, per_grain, 2 * ROWS, lanes), jnp.bfloat16),
            vmem((blocks, 2 * lanes, lanes), jnp.bfloat16),
            vmem((grains, per_grain, ROWS, lanes), f32),
            vmem((blocks, lanes), f32),
            vmem((tiles * cells, lanes), f32),
            vmem((grains, ROWS, lanes), f32),
            vmem((grains, ROWS, lanes), f32),
            vmem((grains, ROWS, lanes), f32),
            vmem((grains, ROWS, lanes), f32),
            vmem((grains, ROWS, lanes), f32),
            vmem((grains, lanes), jnp.int32),
            pltpu.SMEM((grains, lanes), jnp.int32),
            vmem((STEPS, tiles, cells, lanes), f32),
            vmem((STEPS, tiles, cells, lanes), f32),
            vmem((STEPS, ITERS, tiles, cells, lanes), f32),
            vmem((STEPS, ITERS, near_count, cells, lanes), f32),
            vmem((STEPS, tiles * n_depth, 1, lanes), f32),
            dma((tiles + near_count,)),
            dma((tiles + near_count,)),
            dma((STEPS, tiles)),
            dma((STEPS, tiles)),
            dma((STEPS, ITERS, tiles + near_count)),
            dma((STEPS, ITERS, tiles + near_count)),
            dma((STEPS, tiles * n_depth)),
            dma((STEPS, tiles * n_depth)),
            dma,
            vmem((cells, lanes), f32),
            vmem((cells, lanes), f32),
            dma,
            dma,
        ],
        compiler_params=pltpu.CompilerParams(
            collective_id=0, has_side_effects=True, vmem_limit_bytes=60 * 1024 * 1024
        ),
        name="coupled",
    )(
        fluid_offsets.reshape(3 * cells, lanes),
        source.reshape(cells, lanes),
        jnp.transpose(marker_offsets, (0, 2, 1, 3)),
        jnp.transpose(marker_normals, (0, 2, 1, 3)),
        jnp.transpose(dest_tile, (0, 2, 1)),
        cell_index,
        jnp.transpose(grain_velocity),
        grain_mass[None, :],
    )
    return (pressure.reshape(source.shape), jnp.transpose(speed))


def solution(mesh):
    sizes = tuple(mesh.shape[name] for name in ("flow", "cross", "depth"))
    return jax.shard_map(
        functools.partial(per_device, sizes),
        mesh=mesh,
        in_specs=(
            P(None, "flow", "cross", "depth", None),
            P("flow", "cross", "depth", None),
            P(("flow", "cross", "depth"), None, None, None),
            P(("flow", "cross", "depth"), None, None, None),
            P(("flow", "cross", "depth"), None, None),
            P(("flow", "cross", "depth"), None),
            P(("flow", "cross", "depth"), None),
            P(("flow", "cross", "depth")),
        ),
        out_specs=(P("flow", "cross", "depth", None), P(("flow", "cross", "depth"), None)),
        check_vma=False,
    )
```
